256 devices in a mesh: slab: 8 (over y, core), wall: 32 (over x, z).
Axes of the slice: x: 4, y: 4, z: 8, core: 2. Of those that a mesh axis runs over, the one named last changes fastest.
Arguments:
- flow_state: float32 [64, 5, 262144], P(None, None, ('slab', 'wall')), as said below
- match_elem: int32 [2097152], P(('slab', 'wall')), may hold values from 0 to 1023
- match_coord: int32 [3, 2097152], P(None, ('slab', 'wall')), may hold values from 0 to 15
- match_dest: int32 [2097152, 1], P(('slab', 'wall')), may hold values from 0 to 31; in each aligned block of 8192 rows (0 to 8191, 8192 to 16383, ...) at most 640 rows name the same one
- roughness: float32 [5242880], P(('slab', 'wall')), may hold values from 4 to 30
Outputs:
- rate: float32 [64, 4, 262144], P(None, None, ('slab', 'wall'))
- wall_shear: float32 [2, 5242880], P(None, ('slab', 'wall'))
The draws below stay inside these ranges and needn't reach their ends.
Inputs may be any that keep to these rules, and one draw needn't show every extreme that they name: `flow_state`: density lies between 0.8 and 1.25 and the pressure 0.4 (energy - |momentum|^2 / (2 density)) between 0.6 and 1.6 at every node. `match_dest`: among the rows of one device no wall index is named by more than 640 rows, and in every draw some device names one wall index exactly 640 times.
All inputs are finite; a program needn't handle non-finite values.
Results may differ from the reference program's by a relative error of at most 0.0003.
Values sent between devices are 32-bit elements; how exact they have to be, the bound alone decides.
No kernel may reach another device: no remote copies, remote signals or barrier semaphores. Data moves between devices by JAX's collectives and lax.ppermute only.
A program may use at most 64 MiB of HBM per device.

```python
import math
import jax
import jax.numpy as jnp
import numpy as np
from jax import lax

EX = 4
EY = 2
EZ = 128
RES = 16
NEWTON = 8
E_DEV = 1024
ELEMS = 262144
M_DEV = 8192
MATCH = 2097152
CAP = 640
SLOTS = 5242880
N_SLAB = 8
N_WALL = 32


def draw_flow_state(key, part):
    key_rho, key_vel, key_press = jax.random.split(key, 3)
    grid_shape = (64, ELEMS)
    mass_per_volume = jax.random.uniform(key_rho, grid_shape, jnp.float32, 0.8, 1.25)
    stream_speed_vector = jnp.clip(1.5 * jax.random.normal(key_vel, (3, 64, ELEMS), jnp.float32), -4.5, 4.5)
    normal_stress_level = jax.random.uniform(key_press, grid_shape, jnp.float32, 0.6, 1.6)
    momentum = mass_per_volume[None] * stream_speed_vector
    energy = normal_stress_level / 0.4 + 0.5 * mass_per_volume * jnp.sum(stream_speed_vector * stream_speed_vector, axis=0)
    return jnp.stack([mass_per_volume, momentum[0], momentum[1], momentum[2], energy], axis=1)


def set_ends(entries, own_key, least, top_value):
    longest = entries.shape.index(max(entries.shape))
    spots = []
    for shift in (0, 1):
        where = [jax.random.randint(jax.random.fold_in(own_key, axis), (), 0, length) for axis, length in enumerate(entries.shape)]
        where[longest] = (where[longest] + shift) % entries.shape[longest]
        spots.append(tuple(where))
    return entries.at[spots[0]].set(least).at[spots[1]].set(top_value)


def block_scale(rng, shape, cuts, smallest, high):
    factor_of, own = 1.0, jax.random.fold_in(rng, 6)
    for dim, blocks in cuts:
        draws = jnp.exp(jax.random.uniform(jax.random.fold_in(own, dim), (blocks,), jnp.float32, smallest / len(cuts), high / len(cuts)))
        factor_of = factor_of * jnp.repeat(draws, shape[dim] // blocks).reshape([-1 if axis == dim else 1 for axis in range(len(shape))])
    return factor_of


def assign_block(own_key, own, number, rows, amount, top, reach, skew):
    ranking = jax.random.permutation(own_key, amount)
    packed, common = portions_of(amount, rows * top, reach, skew, True), portions_of(amount, rows * top, reach, skew, False)
    places = jnp.arange(amount)

    def named(tallies, turn):
        used = int((tallies > 0).sum())
        fixed = max(1, used // 4)
        passed = fixed + (places - fixed + turn * (used - fixed)) % max(1, amount - fixed)
        return jnp.zeros((amount,), jnp.int32).at[ranking[jnp.where(places < fixed, places, passed)]].set(jnp.asarray(tallies, jnp.int32))

    tallies = jnp.where(number % 4 == 0, named(packed, number // 4), named(common, number - number // 4 - 1))
    mixed = jax.random.permutation(jax.random.fold_in(own, 3), amount)
    donor, receiver = mixed[0:amount // 2 * 2:2], mixed[1:amount // 2 * 2:2]
    margin = jnp.minimum(tallies[donor] - 1, reach - tallies[receiver]) // 2
    margin = jnp.where((donor == ranking[0]) | (receiver == ranking[0]) | (tallies[receiver] == 0), 0, jnp.maximum(margin, 0))
    passed = jax.random.randint(jax.random.fold_in(own, 4), (amount // 2,), 0, 1 << 20) % (margin + 1)
    tallies = tallies.at[donor].add(-passed).at[receiver].add(passed)
    labels = jnp.searchsorted(jnp.cumsum(tallies), jnp.arange(rows * top), side="right").astype(jnp.int32)
    table = labels.reshape(top, rows).T
    table = table[jax.random.permutation(jax.random.fold_in(own, 1), rows)]
    turn = jax.random.randint(jax.random.fold_in(own, 2), (rows, 1), 0, top)
    return jnp.take_along_axis(table, (jnp.arange(top)[None, :] + turn) % top, axis=1)


def portions_of(count, total, reach, lean, full):
    loads = [(1 << 20) // math.isqrt(grade ** lean) + 1 for grade in range(1, count + 1)]
    largest = reach if full else min(reach, max(-(-total // count), total * loads[0] // sum(loads)))
    least = 1 if total - largest >= count - 1 else 0
    counts, spare = [largest] + [least] * (count - 1), total - largest - least * (count - 1)
    while spare > 0:
        free = [i for i in range(1, count) if counts[i] < largest] or [i for i in range(1, count) if counts[i] < reach]
        pool, left = sum([loads[i] for i in free]), spare
        for i in free:
            extra = min(reach - counts[i], max(1, left * loads[i] // pool), spare)
            counts[i] = counts[i] + extra
            spare = spare - extra
    return np.array(counts)


def setup_inputs(seed: int = 0) -> dict:
    keys = jax.random.split(jax.random.key(seed), 6)
    flow_state = draw_flow_state(jax.random.fold_in(keys[5], 71), 0)
    match_elem = set_ends(jax.random.randint(keys[1], (MATCH,), 0, E_DEV), jax.random.fold_in(keys[1], 1), 0, E_DEV - 1).astype(jnp.int32)
    match_coord = set_ends(jax.random.randint(keys[2], (3, MATCH), 0, RES), jax.random.fold_in(keys[2], 1), 0, RES - 1).astype(jnp.int32)
    match_dest_keys = jax.random.split(jax.random.fold_in(keys[3], 1), MATCH // M_DEV)
    match_dest_turns = jax.random.permutation(jax.random.fold_in(keys[3], 3), MATCH // M_DEV)
    match_dest = jax.vmap(lambda own, number: assign_block(jax.random.fold_in(keys[3], 2), own, number, M_DEV, N_WALL, 1, CAP, 1))(match_dest_keys, match_dest_turns).reshape((MATCH, 1))
    roughness = jnp.clip(jnp.exp(math.log(30.0) - 2.014903 * jax.random.uniform(keys[4], (SLOTS,), jnp.float32) ** block_scale(keys[4], (SLOTS,), ((0, 256),), -0.2, 0.2)), 4.0, 30.0)
    return {"flow_state": flow_state, "match_elem": match_elem, "match_coord": match_coord, "match_dest": match_dest, "roughness": roughness}


HIGHEST = lax.Precision.HIGHEST
VISCOSITY = 0.05
FOURIER_LAW_ON = 0.07 / 0.288
KARMAN = 0.41
RELAXATION = 0.35

def gauss_points():
    return np.array([-1.0, -1.0 / np.sqrt(5.0), 1.0 / np.sqrt(5.0), 1.0])

def derivative_tables():
    points = gauss_points()
    bary_weights = np.array([1.0 / np.prod([points[left_index] - points[right_index] for right_index in range(4) if right_index != left_index]) for left_index in range(4)])
    matrix = np.zeros((4, 4))
    for left_index in range(4):
        for right_index in range(4):
            if right_index != left_index:
                matrix[left_index, right_index] = bary_weights[right_index] / bary_weights[left_index] / (points[left_index] - points[right_index])
        matrix[left_index, left_index] = -np.sum(matrix[left_index])
    identity = np.eye(4)
    along_x = np.kron(np.kron(matrix, identity), identity)
    along_y = np.kron(np.kron(identity, matrix), identity)
    along_z = np.kron(np.kron(identity, identity), matrix)
    gradient_table = np.concatenate([along_x, along_y, along_z], axis=0)
    divergence_table = np.concatenate([along_x, along_y, along_z], axis=1)
    return (jnp.asarray(gradient_table, jnp.float32), jnp.asarray(divergence_table, jnp.float32))

def entropy_vars(flow_block, comp_axis):
    mass_per_volume = lax.index_in_dim(flow_block, 0, comp_axis, keepdims=False)
    momentum_x = lax.index_in_dim(flow_block, 1, comp_axis, keepdims=False)
    momentum_y = lax.index_in_dim(flow_block, 2, comp_axis, keepdims=False)
    momentum_z = lax.index_in_dim(flow_block, 3, comp_axis, keepdims=False)
    energy = lax.index_in_dim(flow_block, 4, comp_axis, keepdims=False)
    speed_sq = momentum_x * momentum_x + momentum_y * momentum_y + momentum_z * momentum_z
    normal_stress_level = 0.4 * (energy - 0.5 * speed_sq / mass_per_volume)
    entropy_s = jnp.log(normal_stress_level) - 1.4 * jnp.log(mass_per_volume)
    leading = (1.4 - entropy_s) / 0.4 - 0.5 * speed_sq / (mass_per_volume * normal_stress_level)
    return jnp.stack([leading, momentum_x / normal_stress_level, momentum_y / normal_stress_level, momentum_z / normal_stress_level, -mass_per_volume / normal_stress_level], comp_axis)

def face_terms(field_view, node_axis, elem_axis, lower_edge, upper_edge):
    lower_face = lax.index_in_dim(field_view, 0, node_axis, keepdims=False)
    upper_face = lax.index_in_dim(field_view, 3, node_axis, keepdims=False)
    extent = lower_face.shape[elem_axis]
    next_lower = jnp.concatenate([lax.slice_in_dim(lower_face, 1, extent, axis=elem_axis), upper_edge], elem_axis)
    prev_upper = jnp.concatenate([lower_edge, lax.slice_in_dim(upper_face, 0, extent - 1, axis=elem_axis)], elem_axis)
    add_lower = -3.0 * (prev_upper - lower_face)
    add_upper = 3.0 * (next_lower - upper_face)
    nothing = jnp.zeros_like(lower_face)
    return jnp.stack([add_lower, nothing, nothing, add_upper], node_axis)

def own_terms(field_view, node_axis, elem_axis):
    lower_face = lax.index_in_dim(field_view, 0, node_axis, keepdims=False)
    upper_face = lax.index_in_dim(field_view, 3, node_axis, keepdims=False)
    extent = lower_face.shape[elem_axis]
    return face_terms(field_view, node_axis, elem_axis, lax.slice_in_dim(lower_face, 0, 1, axis=elem_axis), lax.slice_in_dim(upper_face, extent - 1, extent, axis=elem_axis))

def edge_packs(field_x, field_z):
    lower_x = field_x[0]
    upper_x = field_x[3]
    pack_x = jnp.stack([lower_x[:, :, :, 0], upper_x[:, :, :, -1]], 0)
    lower_z = field_z[:, :, 0]
    upper_z = field_z[:, :, 3]
    pack_z = jnp.stack([lower_z[..., 0], upper_z[..., -1]], 0)
    return (pack_x, pack_z)

def viscous_flux(flow_block, entropy_view, edge_faces, tables):
    elem_count = EX * EY * EZ
    nodal_derivs = jnp.dot(tables[0], entropy_view.reshape(64, 5 * elem_count), precision=HIGHEST, preferred_element_type=jnp.float32).reshape(3, 4, 4, 4, 5, EX, EY, EZ)
    lower_x, upper_x, lower_z, upper_z = edge_faces
    recovered_slopes = [nodal_derivs[0] + face_terms(entropy_view, 0, 3, lower_x, upper_x), nodal_derivs[1] + own_terms(entropy_view, 1, 4), nodal_derivs[2] + face_terms(entropy_view, 2, 5, lower_z, upper_z)]
    conserved = flow_block.reshape(4, 4, 4, 5, EX, EY, EZ)
    mass_per_volume = conserved[:, :, :, 0]
    stream_speed_vector = [conserved[:, :, :, 1] / mass_per_volume, conserved[:, :, :, 2] / mass_per_volume, conserved[:, :, :, 3] / mass_per_volume]
    speed_sq = mass_per_volume * (stream_speed_vector[0] * stream_speed_vector[0] + stream_speed_vector[1] * stream_speed_vector[1] + stream_speed_vector[2] * stream_speed_vector[2])
    normal_stress_level = 0.4 * (conserved[:, :, :, 4] - 0.5 * speed_sq)
    kelvin_level = normal_stress_level / mass_per_volume
    strain_rate_tensor = [[kelvin_level * (recovered_slopes[coordinate_heading][:, :, :, 1 + matrix_entry_position] + stream_speed_vector[matrix_entry_position] * recovered_slopes[coordinate_heading][:, :, :, 4]) for matrix_entry_position in range(3)] for coordinate_heading in range(3)]
    divergence = strain_rate_tensor[0][0] + strain_rate_tensor[1][1] + strain_rate_tensor[2][2]
    fluxes = []
    for coordinate_heading in range(3):
        stress = []
        for matrix_entry_position in range(3):
            stress_entry = VISCOSITY * (strain_rate_tensor[coordinate_heading][matrix_entry_position] + strain_rate_tensor[matrix_entry_position][coordinate_heading])
            if matrix_entry_position == coordinate_heading:
                stress_entry = stress_entry - 2.0 / 3.0 * VISCOSITY * divergence
            stress.append(stress_entry)
        enthalpy_transport = FOURIER_LAW_ON * kelvin_level * kelvin_level * recovered_slopes[coordinate_heading][:, :, :, 4]
        energy_flux = stream_speed_vector[0] * stress[0] + stream_speed_vector[1] * stress[1] + stream_speed_vector[2] * stress[2] + enthalpy_transport
        fluxes.append(jnp.stack([stress[0], stress[1], stress[2], energy_flux], 3))
    return fluxes

def residual_rate(fluxes, edge_faces, stress_rows, tables):
    elem_count = EX * EY * EZ
    stacked = jnp.stack(fluxes, 0).reshape(192, 4 * elem_count)
    rate_field = jnp.dot(tables[1], stacked, precision=HIGHEST, preferred_element_type=jnp.float32).reshape(4, 4, 4, 4, EX, EY, EZ)
    lower_x, upper_x, lower_z, upper_z = edge_faces
    rate_field = rate_field + face_terms(fluxes[0], 0, 3, lower_x, upper_x) + own_terms(fluxes[1], 1, 4) + face_terms(fluxes[2], 2, 5, lower_z, upper_z)
    shear_rows = stress_rows.reshape(2, 4, 4, EX, EZ)
    bottom = fluxes[1][:, 0, :, :, :, 0, :]
    rate_field = rate_field.at[:, 0, :, 0, :, 0, :].add(6.0 * (bottom[:, :, 0] - shear_rows[0]))
    rate_field = rate_field.at[:, 0, :, 2, :, 0, :].add(6.0 * (bottom[:, :, 2] - shear_rows[1]))
    return rate_field.reshape(64, 4, elem_count)

def lagrange_rows(coordinate):
    points = gauss_points()
    rows_out = []
    for left_index in range(4):
        factor_prod = jnp.ones_like(coordinate)
        for right_index in range(4):
            if right_index != left_index:
                factor_prod = factor_prod * (coordinate - float(points[right_index])) / float(points[left_index] - points[right_index])
        rows_out.append(factor_prod)
    return jnp.stack(rows_out, 0)

def probe_values(flow_block, elements, coords_int):
    coords = (2.0 * coords_int.astype(jnp.float32) + 1.0) / RES - 1.0
    basis_x = lagrange_rows(coords[0])
    basis_y = lagrange_rows(coords[1])
    basis_z = lagrange_rows(coords[2])
    weights = (basis_x[:, None, None, :] * basis_y[None, :, None, :] * basis_z[None, None, :, :]).reshape(64, -1)
    values = [lax.optimization_barrier(jnp.sum(weights * jnp.take(flow_block[:, matrix_entry_position, :], elements, axis=1), axis=0)) for matrix_entry_position in (0, 1, 3)]
    layer_index = (elements // EZ % EY).astype(jnp.float32)
    return jnp.stack(values + [2.0 * layer_index + 1.0 + coords[1]], 0)

def slot_ranks(destination, wall_count):
    onehot = (destination[None, :] == jnp.arange(wall_count, dtype=jnp.int32)[:, None]).astype(jnp.int32)
    before = jnp.cumsum(onehot, axis=1) - onehot
    return lax.optimization_barrier(jnp.sum(before * onehot, axis=0)).astype(jnp.int32)

def wall_model(mass_per_volume, mom_x, mom_z, height, factor):
    vel_x = mom_x / mass_per_volume
    vel_z = mom_z / mass_per_volume
    slip_speed = jnp.maximum(jnp.sqrt(vel_x * vel_x + vel_z * vel_z), 0.5)
    reynolds = height * slip_speed * mass_per_volume / VISCOSITY
    log_term = jnp.log(factor * reynolds)
    newton_ratio = jnp.ones_like(mass_per_volume)
    for sweep_index in range(NEWTON):
        residue = newton_ratio - (log_term - jnp.log(newton_ratio)) / KARMAN
        newton_slope = 1.0 + 1.0 / (KARMAN * newton_ratio)
        newton_ratio = newton_ratio - RELAXATION * residue / newton_slope
    friction = slip_speed / newton_ratio
    stress_scale = mass_per_volume * friction * friction / slip_speed
    return (stress_scale * vel_x, stress_scale * vel_z)

def reference(flow_state, match_elem, match_coord, match_dest, roughness):
    tables = derivative_tables()
    devices = N_SLAB * N_WALL
    destination_all = match_dest[:, 0]

    def block_of(device):
        return lax.dynamic_slice_in_dim(flow_state, device * E_DEV, E_DEV, axis=2)

    def rows_of(source, device):
        return lax.dynamic_slice_in_dim(source, device * M_DEV, M_DEV, axis=source.ndim - 1)

    def neighbours(device):
        slab_pos = device // N_WALL
        wall_pos = device % N_WALL
        prev_x = (slab_pos + N_SLAB - 1) % N_SLAB * N_WALL + wall_pos
        next_x = (slab_pos + 1) % N_SLAB * N_WALL + wall_pos
        prev_z = slab_pos * N_WALL + (wall_pos + N_WALL - 1) % N_WALL
        next_z = slab_pos * N_WALL + (wall_pos + 1) % N_WALL
        return (prev_x, next_x, prev_z, next_z)

    def edges_from(packs_x, packs_z, device):
        prev_x, next_x, prev_z, next_z = neighbours(device)
        return (packs_x[prev_x][1][:, :, :, None], packs_x[next_x][0][:, :, :, None], packs_z[prev_z][1][..., None], packs_z[next_z][0][..., None])

    def first_pass(device, loop_carry):
        packs_x, packs_z, probes, slots = loop_carry
        device = device.astype(jnp.int32)
        flow_block = block_of(device)
        entropy_view = entropy_vars(flow_block, 1).reshape(4, 4, 4, 5, EX, EY, EZ)
        pack_x, pack_z = edge_packs(entropy_view, entropy_view)
        probe_rows = probe_values(flow_block, rows_of(match_elem, device), rows_of(match_coord, device))
        destination = rows_of(destination_all, device)
        slot_rank = slot_ranks(destination, N_WALL)
        slot_index = (device // N_WALL * N_WALL + destination) * (N_WALL * CAP) + device % N_WALL * CAP + slot_rank
        return (packs_x.at[device].set(pack_x), packs_z.at[device].set(pack_z), lax.dynamic_update_slice_in_dim(probes, probe_rows, device * M_DEV, axis=1), lax.dynamic_update_slice_in_dim(slots, slot_index.astype(jnp.int32), device * M_DEV, axis=0))
    start_carry = (jnp.zeros((devices, 2, 4, 4, 5, EY, EZ), jnp.float32), jnp.zeros((devices, 2, 4, 4, 5, EX, EY), jnp.float32), jnp.zeros((4, MATCH), jnp.float32), jnp.zeros((MATCH,), jnp.int32))
    packs_x, packs_z, probes, slots = lax.fori_loop(0, devices, first_pass, start_carry)
    slot_data = jnp.zeros((4, SLOTS), jnp.float32).at[:, slots].set(probes)
    occupied = slot_data[0] > 0.0
    mass_per_volume = jnp.where(occupied, slot_data[0], 1.0)
    height = jnp.where(occupied, slot_data[3], 1.0)
    stress_x, stress_z = wall_model(mass_per_volume, slot_data[1], slot_data[2], height, roughness)
    wall_shear = jnp.where(occupied[None, :], jnp.stack([stress_x, stress_z], 0), 0.0)

    def flux_of(device):
        flow_block = block_of(device)
        entropy_view = entropy_vars(flow_block, 1).reshape(4, 4, 4, 5, EX, EY, EZ)
        return viscous_flux(flow_block, entropy_view, edges_from(packs_x, packs_z, device), tables)

    def second_pass(device, loop_carry):
        flux_x, flux_z = loop_carry
        device = device.astype(jnp.int32)
        fluxes = flux_of(device)
        pack_x, pack_z = edge_packs(fluxes[0], fluxes[2])
        return (flux_x.at[device].set(pack_x), flux_z.at[device].set(pack_z))
    flux_x, flux_z = lax.fori_loop(0, devices, second_pass, (jnp.zeros((devices, 2, 4, 4, 4, EY, EZ), jnp.float32), jnp.zeros((devices, 2, 4, 4, 4, EX, EY), jnp.float32)))

    def third_pass(device, rate_all):
        device = device.astype(jnp.int32)
        fluxes = flux_of(device)
        stress_rows = wall_shear[:, rows_of(slots, device)]
        rate_field = residual_rate(fluxes, edges_from(flux_x, flux_z, device), stress_rows, tables)
        return lax.dynamic_update_slice_in_dim(rate_all, rate_field, device * E_DEV, axis=2)
    rate_all = lax.fori_loop(0, devices, third_pass, jnp.zeros((64, 4, ELEMS), jnp.float32))
    return (rate_all, wall_shear)
```

```python
import jax
import jax.numpy as jnp
import numpy as np
from jax import lax
from jax.experimental import pallas as pl
from jax.experimental.pallas import tpu as pltpu
from jax.sharding import PartitionSpec as P

EX = 4
EY = 2
EZ = 128
RES = 16
NEWTON = 8
CAP = 640
N_WALL = 32
M_DEV = 8192

VISCOSITY = 0.05
FOURIER_LAW_ON = 0.07 / 0.288
KARMAN = 0.41
RELAXATION = 0.35
F32 = jnp.float32
BF16 = jnp.bfloat16


def gauss_points():
    return np.array([-1.0, -1.0 / np.sqrt(5.0), 1.0 / np.sqrt(5.0), 1.0])


def derivative_matrix():
    points = gauss_points()
    bary = [
        1.0 / np.prod([points[i] - points[j] for j in range(4) if j != i]) for i in range(4)
    ]
    matrix = np.zeros((4, 4))
    for i in range(4):
        for j in range(4):
            if i != j:
                matrix[i, j] = bary[j] / bary[i] / (points[i] - points[j])
        matrix[i, i] = -np.sum(matrix[i])
    return matrix


D = derivative_matrix()
EVEN0 = float(0.5 * (D[0, 0] + D[0, 3]))
EVEN1 = float(0.5 * (D[1, 0] + D[1, 3]))
ODD00 = float(0.5 * (D[0, 0] - D[0, 3]))
ODD01 = float(0.5 * (D[0, 1] - D[0, 2]))
ODD10 = float(0.5 * (D[1, 0] - D[1, 3]))
ODD11 = float(0.5 * (D[1, 1] - D[1, 2]))


def line_derivative(u0, u1, u2, u3):
    even = (u0 + u3) - (u1 + u2)
    odd0 = u0 - u3
    odd1 = u1 - u2
    half0 = EVEN0 * even
    half1 = EVEN1 * even
    mean0 = ODD00 * odd0 + ODD01 * odd1
    mean1 = ODD10 * odd0 + ODD11 * odd1
    return mean0 + half0, mean1 + half1, mean1 - half1, mean0 - half0


def iota(shape, dim):
    return lax.broadcasted_iota(jnp.int32, shape, dim)


def entropy_of(rho, mx, my, mz, energy):
    inv_rho = 1.0 / rho
    speed_sq = mx * mx + my * my + mz * mz
    pressure = 0.4 * (energy - 0.5 * speed_sq * inv_rho)
    entropy_s = jnp.log(pressure) - 1.4 * jnp.log(rho)
    inv_p = 1.0 / pressure
    leading = (1.4 - entropy_s) / 0.4 - 0.5 * speed_sq * inv_rho * inv_p
    return leading, mx * inv_p, my * inv_p, mz * inv_p, -rho * inv_p


def line_nodes(direction, line):
    outer, inner = line // 4, line % 4
    if direction == 0:
        return [16 * a + 4 * outer + inner for a in range(4)]
    if direction == 1:
        return [16 * outer + 4 * b + inner for b in range(4)]
    return [16 * outer + 4 * inner + c for c in range(4)]


def pack_x(get_lower, get_upper, up_ref, low_ref):
    pair = iota((8, 128), 0) // 2
    for block in range(16):
        upper = pltpu.roll(get_upper(4 * block), 2, 0)
        lower = get_lower(4 * block)
        for i in range(1, 4):
            upper = jnp.where(pair == i, pltpu.roll(get_upper(4 * block + i), (2 + 2 * i) % 8, 0), upper)
            lower = jnp.where(pair == i, pltpu.roll(get_lower(4 * block + i), 2 * i, 0), lower)
        up_ref[pl.ds(8 * block, 8), :] = upper
        low_ref[pl.ds(8 * block, 8), :] = lower


def pack_z(get_lower, get_upper, up_ref, low_ref):
    lane = iota((8, 128), 1)
    upper = jnp.zeros((8, 128), F32)
    lower = jnp.zeros((8, 128), F32)
    for k in range(64):
        upper = jnp.where(lane == k, pltpu.roll(get_upper(k), (k + 1) % 128, 1), upper)
        low = get_lower(k)
        lower = jnp.where(lane == k, low if k == 0 else pltpu.roll(low, k, 1), lower)
    up_ref[...] = upper
    low_ref[...] = lower


def entropy_kernel(flow_ref, v_ref, xup_ref, xlow_ref, zup_ref, zlow_ref):
    for n in range(64):
        tile, sub = n // 8, n % 8
        state = [flow_ref[pl.ds(c * 512 + tile * 64 + sub, 8, stride=8), :] for c in range(5)]
        values = entropy_of(*state)
        for k in range(4):
            v_ref[k * 64 + n] = values[1 + k]

    def face(direction, end):
        return lambda k: v_ref[(k // 16) * 64 + line_nodes(direction, k % 16)[end]]

    pack_x(face(0, 0), face(0, 3), xup_ref, xlow_ref)
    pack_z(face(2, 0), face(2, 3), zup_ref, zlow_ref)


def flux_kernel(v_ref, xprev_ref, xnext_ref, zprev_ref, znext_ref,
                rate_ref, xup_ref, xlow_ref, zup_ref, zlow_ref, g_ref, f_ref):
    row = iota((8, 128), 0)
    lane = iota((8, 128), 1)
    odd = row % 2 == 1

    def jumps_y(lower, upper):
        prev = jnp.where(odd, pltpu.roll(upper, 1, 0), lower)
        following = jnp.where(odd, upper, pltpu.roll(lower, 7, 0))
        return prev, following

    for k in range(64):
        comp, line = k // 16, k % 16
        for direction in range(3):
            nodes = line_nodes(direction, line)
            u = [v_ref[comp * 64 + n] for n in nodes]
            d = list(line_derivative(*u))
            if direction == 0:
                i = k % 4
                prev_halo = xprev_ref[pl.ds(8 * (k // 4), 8), :]
                next_halo = xnext_ref[pl.ds(8 * (k // 4), 8), :]
                if i:
                    prev_halo = pltpu.roll(prev_halo, 8 - 2 * i, 0)
                if i != 3:
                    next_halo = pltpu.roll(next_halo, 6 - 2 * i, 0)
                prev = jnp.where(row < 2, prev_halo, pltpu.roll(u[3], 2, 0))
                following = jnp.where(row >= 6, next_halo, pltpu.roll(u[0], 6, 0))
            elif direction == 1:
                prev, following = jumps_y(u[0], u[3])
            else:
                prev_halo = zprev_ref[...]
                if k:
                    prev_halo = pltpu.roll(prev_halo, 128 - k, 1)
                next_halo = pltpu.roll(znext_ref[...], 127 - k, 1)
                prev = jnp.where(lane == 0, prev_halo, pltpu.roll(u[3], 1, 1))
                following = jnp.where(lane == 127, next_halo, pltpu.roll(u[0], 127, 1))
            d[0] = d[0] - 3.0 * (prev - u[0])
            d[3] = d[3] + 3.0 * (following - u[3])
            for end in range(4):
                g_ref[(direction * 4 + comp) * 64 + nodes[end]] = d[end]

    def pointwise(n, carry):
        v = [v_ref[c * 64 + n] for c in range(4)]
        g = [[g_ref[(d * 4 + c) * 64 + n] for c in range(4)] for d in range(3)]
        temperature = -1.0 / v[3]
        u = [v[i] * temperature for i in range(3)]
        scaled = VISCOSITY * temperature
        gu = [[scaled * (g[d][i] + u[i] * g[d][3]) for i in range(3)] for d in range(3)]
        third = (2.0 / 3.0) * (gu[0][0] + gu[1][1] + gu[2][2])
        conduct = FOURIER_LAW_ON * temperature * temperature
        tau = [[None] * 3 for _ in range(3)]
        for d in range(3):
            for i in range(d, 3):
                entry = gu[d][i] + gu[i][d]
                if i == d:
                    entry = entry - third
                tau[d][i] = entry
                tau[i][d] = entry
        for d in range(3):
            heat = u[0] * tau[d][0] + u[1] * tau[d][1] + u[2] * tau[d][2] + conduct * g[d][3]
            for c in range(3):
                f_ref[(d * 4 + c) * 64 + n] = tau[d][c]
            f_ref[(d * 4 + 3) * 64 + n] = heat
        return carry

    lax.fori_loop(0, 64, pointwise, 0, unroll=4)

    def face(direction, end):
        return lambda k: f_ref[(direction * 4 + k // 16) * 64 + line_nodes(direction, k % 16)[end]]

    pack_x(face(0, 0), face(0, 3), xup_ref, xlow_ref)
    pack_z(face(2, 0), face(2, 3), zup_ref, zlow_ref)

    for direction in range(3):
        for k in range(64):
            comp, line = k // 16, k % 16
            nodes = line_nodes(direction, line)
            u = [f_ref[(direction * 4 + comp) * 64 + n] for n in nodes]
            d = list(line_derivative(*u))
            if direction == 0:
                prev = jnp.where(row < 2, 0.0, pltpu.roll(u[3], 2, 0))
                following = jnp.where(row >= 6, 0.0, pltpu.roll(u[0], 6, 0))
            elif direction == 1:
                prev, following = jumps_y(u[0], u[3])
            else:
                prev = jnp.where(lane == 0, 0.0, pltpu.roll(u[3], 1, 1))
                following = jnp.where(lane == 127, 0.0, pltpu.roll(u[0], 127, 1))
            d[0] = d[0] - 3.0 * (prev - u[0])
            d[3] = d[3] + 3.0 * (following - u[3])
            if direction == 1 and comp in (0, 2):
                d[0] = d[0] + jnp.where(odd, 0.0, 6.0 * u[0])
            for end in range(4):
                where = comp * 64 + nodes[end]
                if direction == 0:
                    rate_ref[where] = d[end]
                else:
                    rate_ref[where] = rate_ref[where] + d[end]


def rate_kernel(part_ref, xprev_ref, xnext_ref, zprev_ref, znext_ref, shear_ref, rate_ref):
    row = iota((8, 128), 0)
    lane = iota((8, 128), 1)
    for n in range(64):
        a, b, c = n // 16, n // 4 % 4, n % 4
        for comp in range(4):
            total = part_ref[comp * 64 + n]
            if a in (0, 3):
                k = comp * 16 + 4 * b + c
                i = k % 4
                halo = (xprev_ref if a == 0 else xnext_ref)[pl.ds(8 * (k // 4), 8), :]
                shift = (8 - 2 * i) % 8 if a == 0 else 6 - 2 * i
                if shift:
                    halo = pltpu.roll(halo, shift, 0)
                if a == 0:
                    total = total - jnp.where(row < 2, 3.0 * halo, 0.0)
                else:
                    total = total + jnp.where(row >= 6, 3.0 * halo, 0.0)
            if c in (0, 3):
                k = comp * 16 + 4 * a + b
                halo = (zprev_ref if c == 0 else znext_ref)[...]
                shift = (128 - k) % 128 if c == 0 else 127 - k
                if shift:
                    halo = pltpu.roll(halo, shift, 1)
                if c == 0:
                    total = total - jnp.where(lane == 0, 3.0 * halo, 0.0)
                else:
                    total = total + jnp.where(lane == 127, 3.0 * halo, 0.0)
            if b == 0 and comp in (0, 2):
                total = total - 6.0 * shear_ref[(comp // 2) * 16 + 4 * a + c]
            rate_ref[pl.ds(n * 32 + comp, 8, stride=4), :] = total


PROBE_BLOCK = 512


def probe_kernel(flow_ref, elem_ref, coord_ref, dest_ref, probe_ref, rank_ref, lhs_ref):
    points = gauss_points()
    for part, comp in enumerate((0, 1, 3)):
        value = flow_ref[comp]
        high = value.astype(BF16)
        lhs_ref[pl.ds(64 * part, 64), :] = high
        lhs_ref[pl.ds(192 + 64 * part, 64), :] = (value - high.astype(F32)).astype(BF16)

    before = (iota((128, 128), 0) < iota((128, 128), 1)).astype(F32).astype(BF16)
    counter = jnp.concatenate([before, jnp.ones((128, 128), BF16)], axis=1)
    wall_ids = iota((N_WALL, 128), 0)

    def rank_block(block, total):
        dest = dest_ref[0:1, pl.ds(pl.multiple_of(block * 128, 128), 128)]
        hot = (wall_ids == dest).astype(F32)
        counts = jnp.dot(hot.astype(BF16), counter, preferred_element_type=F32)
        rank = jnp.sum(hot * (counts[:, :128] + total), axis=0, keepdims=True)
        rank_ref[pl.ds(block, 1), :] = rank.astype(jnp.int32)
        return total + counts[:, 128:]

    lax.fori_loop(0, M_DEV // 128, rank_block, jnp.zeros((N_WALL, 128), F32), unroll=4)

    def basis_rows(coordinate, index):
        product = jnp.ones_like(coordinate)
        scale = 1.0
        for other in range(4):
            node = float(points[other])
            product = product * jnp.where(index == other, 1.0, coordinate - node)
        scales = [
            float(1.0 / np.prod([points[i] - points[j] for j in range(4) if j != i])) for i in range(4)
        ]
        scale = jnp.where(
            index == 0, scales[0], jnp.where(index == 1, scales[1], jnp.where(index == 2, scales[2], scales[3]))
        )
        return product * scale

    width = PROBE_BLOCK
    elem_ids = iota((1024, width), 0)
    row16 = iota((16, width), 0)

    def probe_block(block, carry):
        start = pl.multiple_of(block * width, width)
        elem = elem_ref[0:1, pl.ds(start, width)]
        hot = (elem_ids == elem).astype(F32).astype(BF16)
        picked = jnp.dot(lhs_ref[...], hot, preferred_element_type=F32)
        coords = [
            (2.0 * coord_ref[d : d + 1, pl.ds(start, width)].astype(F32) + 1.0) / RES - 1.0 for d in range(3)
        ]
        wide = [jnp.broadcast_to(coords[d], (16, width)) for d in range(3)]
        along_yz = basis_rows(wide[1], row16 // 4) * basis_rows(wide[2], row16 % 4)
        along_x = [basis_rows(wide[0], jnp.full((16, width), a, jnp.int32)) for a in range(4)]
        for part in range(3):
            total = None
            for a in range(4):
                base = 64 * part + 16 * a
                term = along_x[a] * (picked[base : base + 16] + picked[192 + base : 192 + base + 16])
                total = term if total is None else total + term
            value = jnp.sum(total * along_yz, axis=0, keepdims=True)
            for i in range(width // 128):
                probe_ref[part, pl.ds(block * (width // 128) + i, 1), :] = value[:, 128 * i : 128 * (i + 1)]
        layer = (elem // EZ % EY).astype(F32)
        height = 2.0 * layer + 1.0 + coords[1]
        for i in range(width // 128):
            probe_ref[3, pl.ds(block * (width // 128) + i, 1), :] = height[:, 128 * i : 128 * (i + 1)]
        return carry

    lax.fori_loop(0, M_DEV // width, probe_block, 0)


def wall_model(mass_per_volume, mom_x, mom_z, height, factor):
    vel_x = mom_x / mass_per_volume
    vel_z = mom_z / mass_per_volume
    slip_speed = jnp.maximum(jnp.sqrt(vel_x * vel_x + vel_z * vel_z), 0.5)
    reynolds = height * slip_speed * mass_per_volume / VISCOSITY
    log_term = jnp.log(factor * reynolds)
    newton_ratio = jnp.ones_like(mass_per_volume)
    for sweep_index in range(NEWTON):
        residue = newton_ratio - (log_term - jnp.log(newton_ratio)) / KARMAN
        newton_slope = 1.0 + 1.0 / (KARMAN * newton_ratio)
        newton_ratio = newton_ratio - RELAXATION * residue / newton_slope
    friction = slip_speed / newton_ratio
    stress_scale = mass_per_volume * friction * friction / slip_speed
    return (stress_scale * vel_x, stress_scale * vel_z)


WALL_BLOCK = 1024


def wall_kernel(probe_ref, rank_ref, dest_ref, rough_ref, slots_ref, shear_ref, lhs_ref, hot_ref):
    rows = M_DEV // 128
    rank = rank_ref[...]
    dest = dest_ref[...]
    lane = rank % 128
    table_row = dest * (CAP // 128) + rank // 128

    def pick(r, total):
        entry = jnp.broadcast_to(rough_ref[pl.ds(r, 1), :], (rows, 128))
        entry = jnp.take_along_axis(entry, lane, axis=1, mode="promise_in_bounds")
        return jnp.where(table_row == r, entry, total)

    factor = lax.fori_loop(0, CAP * N_WALL // 128, pick, jnp.ones((rows, 128), F32), unroll=4)
    shear = wall_model(probe_ref[0], probe_ref[1], probe_ref[2], probe_ref[3], factor)

    shear_ref[...] = jnp.zeros_like(shear_ref)
    parts = []
    for comp in range(2):
        for pair in range(16):
            shear_ref[pl.ds(128 * comp + 8 * pair, 4, stride=2), :] = shear[comp][4 * pair : 4 * pair + 4]
        high = shear[comp].astype(BF16).astype(F32)
        parts += [high, shear[comp] - high]

    code = (rank // 256) * N_WALL + dest
    low = rank % 256
    code_ids = iota((96, 128), 0)
    low_ids = iota((256, 128), 0)
    total = jnp.zeros((384, 256), F32)
    per = WALL_BLOCK // 128
    for block in range(M_DEV // WALL_BLOCK):
        for i in range(per):
            r = block * per + i
            match = code_ids == code[r : r + 1]
            for part in range(4):
                lhs_ref[pl.ds(96 * part, 96), pl.ds(128 * r, 128)] = jnp.where(
                    match, parts[part][r : r + 1], 0.0
                ).astype(BF16)
            hot_ref[:, pl.ds(128 * r, 128)] = (low_ids == low[r : r + 1]).astype(F32).astype(BF16)
        span = pl.ds(block * WALL_BLOCK, WALL_BLOCK)
        total = total + lax.dot_general(
            lhs_ref[:, span], hot_ref[:, span], (((1,), (1,)), ((), ())), preferred_element_type=F32
        )
    for comp in range(2):
        both = total[192 * comp : 192 * comp + 96] + total[192 * comp + 96 : 192 * comp + 192]
        for chunk in range(CAP // 128):
            q, half = chunk // 2, chunk % 2
            for w in range(0, N_WALL, 8):
                slots_ref[pl.ds(w * 10 + chunk * 2 + comp, 8, stride=10), :] = both[
                    q * N_WALL + w : q * N_WALL + w + 8, 128 * half : 128 * half + 128
                ]


VMEM = pl.BlockSpec(memory_space=pltpu.VMEM)


def call(kernel, inputs, outputs, scratch=(), name=None):
    return pl.pallas_call(
        kernel,
        out_shape=[jax.ShapeDtypeStruct(shape, dtype) for shape, dtype in outputs],
        in_specs=[VMEM] * len(inputs),
        out_specs=[VMEM] * len(outputs),
        scratch_shapes=[pltpu.VMEM(shape, dtype) for shape, dtype in scratch],
        name=name,
        compiler_params=pltpu.CompilerParams(vmem_limit_bytes=40 * 1024 * 1024),
    )(*inputs)


def ring(axis, step):
    count = lax.axis_size(axis)
    return [(i, (i + step) % count) for i in range(count)]


def exchange(xup, xlow, zup, zlow):
    return (
        lax.ppermute(xup, "slab", ring("slab", 1)),
        lax.ppermute(xlow, "slab", ring("slab", -1)),
        lax.ppermute(zup, "wall", ring("wall", 1)),
        lax.ppermute(zlow, "wall", ring("wall", -1)),
    )


def local(flow_state, match_elem, match_coord, match_dest, roughness):
    faces = [((128, 128), F32), ((128, 128), F32), ((8, 128), F32), ((8, 128), F32)]
    flow = flow_state.transpose(1, 0, 2)
    flow_rows = flow.reshape(5, 8, 8, 8, 128).transpose(0, 1, 3, 2, 4).reshape(2560, 128)
    rough = lax.all_to_all(roughness.reshape(N_WALL, 1, CAP), "wall", 0, 0, tiled=True).reshape(160, 128)
    v, *packs = call(entropy_kernel, [flow_rows], [((256, 8, 128), F32)] + faces, name="entropy")
    halos = exchange(*packs)
    probe, rank = call(
        probe_kernel,
        [flow, match_elem.reshape(1, M_DEV), match_coord, match_dest.reshape(1, M_DEV)],
        [((4, 64, 128), F32), ((64, 128), jnp.int32)],
        [((384, 1024), BF16)],
        name="matching",
    )
    part, *packs = call(
        flux_kernel,
        [v, *halos],
        [((256, 8, 128), F32)] + faces,
        [((768, 8, 128), F32), ((768, 8, 128), F32)],
        name="flux",
    )
    halos = exchange(*packs)
    slots, shear = call(
        wall_kernel,
        [probe, rank, match_dest.reshape(64, 128), rough],
        [((320, 128), F32), ((256, 128), F32)],
        [((384, M_DEV), BF16), ((256, M_DEV), BF16)],
        name="wallmodel",
    )
    outgoing = slots.reshape(N_WALL, 5, 2, 128).transpose(2, 0, 1, 3).reshape(2, N_WALL * CAP)
    wall_shear = lax.all_to_all(outgoing, "wall", split_axis=1, concat_axis=1, tiled=True)
    (rate,) = call(
        rate_kernel, [part, *halos, shear.reshape(32, 8, 128)], [((2048, 128), F32)], name="rate"
    )
    rate = rate.reshape(64, 8, 4, 128).transpose(0, 2, 1, 3).reshape(64, 4, 1024)
    return (rate, wall_shear)


def solution(mesh):
    return jax.shard_map(
        local,
        mesh=mesh,
        in_specs=(
            P(None, None, ("slab", "wall")),
            P(("slab", "wall")),
            P(None, ("slab", "wall")),
            P(("slab", "wall"), None),
            P(("slab", "wall")),
        ),
        out_specs=(P(None, None, ("slab", "wall")), P(None, ("slab", "wall"))),
        check_vma=False,
    )
```

```python
import jax
import jax.numpy as jnp
import numpy as np
from jax import lax
from jax.experimental import pallas as pl
from jax.experimental.pallas import tpu as pltpu
from jax.sharding import PartitionSpec as P

EX = 4
EY = 2
EZ = 128
RES = 16
NEWTON = 8
CAP = 640
N_WALL = 32
M_DEV = 8192

VISCOSITY = 0.05
FOURIER_LAW_ON = 0.07 / 0.288
KARMAN = 0.41
RELAXATION = 0.35
F32 = jnp.float32
BF16 = jnp.bfloat16


def gauss_points():
    return np.array([-1.0, -1.0 / np.sqrt(5.0), 1.0 / np.sqrt(5.0), 1.0])


def derivative_matrix():
    points = gauss_points()
    bary = [
        1.0 / np.prod([points[i] - points[j] for j in range(4) if j != i]) for i in range(4)
    ]
    matrix = np.zeros((4, 4))
    for i in range(4):
        for j in range(4):
            if i != j:
                matrix[i, j] = bary[j] / bary[i] / (points[i] - points[j])
        matrix[i, i] = -np.sum(matrix[i])
    return matrix


D = derivative_matrix()
EVEN0 = float(0.5 * (D[0, 0] + D[0, 3]))
EVEN1 = float(0.5 * (D[1, 0] + D[1, 3]))
ODD00 = float(0.5 * (D[0, 0] - D[0, 3]))
ODD01 = float(0.5 * (D[0, 1] - D[0, 2]))
ODD10 = float(0.5 * (D[1, 0] - D[1, 3]))
ODD11 = float(0.5 * (D[1, 1] - D[1, 2]))


def line_derivative(u0, u1, u2, u3):
    even = (u0 + u3) - (u1 + u2)
    odd0 = u0 - u3
    odd1 = u1 - u2
    half0 = EVEN0 * even
    half1 = EVEN1 * even
    mean0 = ODD00 * odd0 + ODD01 * odd1
    mean1 = ODD10 * odd0 + ODD11 * odd1
    return mean0 + half0, mean1 + half1, mean1 - half1, mean0 - half0


def iota(shape, dim):
    return lax.broadcasted_iota(jnp.int32, shape, dim)


def entropy_of(rho, mx, my, mz, energy):
    inv_rho = 1.0 / rho
    speed_sq = mx * mx + my * my + mz * mz
    pressure = 0.4 * (energy - 0.5 * speed_sq * inv_rho)
    entropy_s = jnp.log(pressure) - 1.4 * jnp.log(rho)
    inv_p = 1.0 / pressure
    leading = (1.4 - entropy_s) / 0.4 - 0.5 * speed_sq * inv_rho * inv_p
    return leading, mx * inv_p, my * inv_p, mz * inv_p, -rho * inv_p


def line_nodes(direction, line):
    outer, inner = line // 4, line % 4
    if direction == 0:
        return [16 * a + 4 * outer + inner for a in range(4)]
    if direction == 1:
        return [16 * outer + 4 * b + inner for b in range(4)]
    return [16 * outer + 4 * inner + c for c in range(4)]


def is_even(axis):
    return lax.rem(lax.axis_index(axis), 2) == 0


def pick(condition, one, other):
    return lax.select(jnp.broadcast_to(condition, one.shape), one, other)


def pack_x(get_lower, get_upper, first_ref, second_ref):
    even = is_even("slab")
    pair = iota((8, 128), 0) // 2
    for block in range(16):
        upper = pltpu.roll(get_upper(4 * block), 2, 0)
        lower = get_lower(4 * block)
        for i in range(1, 4):
            upper = jnp.where(pair == i, pltpu.roll(get_upper(4 * block + i), (2 + 2 * i) % 8, 0), upper)
            lower = jnp.where(pair == i, pltpu.roll(get_lower(4 * block + i), 2 * i, 0), lower)
        first_ref[pl.ds(8 * block, 8), :] = pick(even, upper, lower)
        second_ref[pl.ds(8 * block, 8), :] = pick(even, lower, upper)


def pack_z(get_lower, get_upper):
    lane = iota((8, 128), 1)
    upper = jnp.zeros((8, 128), F32)
    lower = jnp.zeros((8, 128), F32)
    for k in range(64):
        upper = jnp.where(lane == k, pltpu.roll(get_upper(k), (k + 1) % 128, 1), upper)
        low = get_lower(k)
        lower = jnp.where(lane == k, low if k == 0 else pltpu.roll(low, k, 1), lower)
    return upper, lower


def x_halos(first_ref, second_ref, block):
    even = is_even("slab")
    first = first_ref[pl.ds(8 * block, 8), :]
    second = second_ref[pl.ds(8 * block, 8), :]
    return pick(even, second, first), pick(even, first, second)


def entropy_kernel(flow_ref, v_ref, table_ref, x1_ref, x2_ref, z1_ref, z2_ref, rows_ref, sems):
    copies = [
        pltpu.make_async_copy(
            flow_ref.at[:, pl.ds(128 * part, 128), :], rows_ref.at[:, pl.ds(128 * part, 128), :], sems.at[part]
        )
        for part in range(4)
    ]
    for copy in copies:
        copy.start()
    for part in range(4):
        copies[part].wait()
        for n in range(16 * part, 16 * part + 16):
            start = n // 8 * 64 + n % 8
            values = entropy_of(*[rows_ref[c, pl.ds(start, 8, stride=8), :] for c in range(5)])
            for k in range(4):
                v_ref[k * 64 + n] = values[1 + k]
        for field, c in enumerate((0, 1, 3)):
            for j in range(8):
                value = jnp.concatenate(
                    [rows_ref[c, pl.ds(part * 128 + half * 64 + j * 8, 8), :] for half in range(2)], axis=0
                )
                high = value.astype(BF16)
                low = (value - high.astype(F32)).astype(BF16)
                base = j // 2 * 384 + field * 64 + part * 16
                lanes = pl.ds(j % 2 * 128, 128)
                table_ref[pl.ds(base, 16), lanes] = high
                table_ref[pl.ds(base + 192, 16), lanes] = low

    def face(direction, end):
        return lambda k: v_ref[(k // 16) * 64 + line_nodes(direction, k % 16)[end]]

    pack_x(face(0, 0), face(0, 3), x1_ref, x2_ref)
    upper, lower = pack_z(face(2, 0), face(2, 3))
    even = is_even("wall")
    z1_ref[...] = pick(even, upper, lower)
    z2_ref[...] = pick(even, lower, upper)


def jumps_y(lower, upper):
    odd = iota((8, 128), 0) % 2 == 1
    prev = jnp.where(odd, pltpu.roll(upper, 1, 0), lower)
    following = jnp.where(odd, upper, pltpu.roll(lower, 7, 0))
    return prev, following


def flux_kernel(v_ref, x1_ref, x2_ref, z1_ref, z2_ref,
                rate_ref, f1_ref, f2_ref, zup_ref, zlow_ref, g_ref, f_ref):
    row = iota((8, 128), 0)
    lane = iota((8, 128), 1)
    odd = row % 2 == 1
    even = is_even("wall")
    z_prev = pick(even, z2_ref[...], z1_ref[...])
    z_next = pick(even, z1_ref[...], z2_ref[...])

    for k in range(64):
        comp, line = k // 16, k % 16
        for direction in range(3):
            nodes = line_nodes(direction, line)
            u = [v_ref[comp * 64 + n] for n in nodes]
            d = list(line_derivative(*u))
            if direction == 0:
                i = k % 4
                prev_halo, next_halo = x_halos(x1_ref, x2_ref, k // 4)
                if i:
                    prev_halo = pltpu.roll(prev_halo, 8 - 2 * i, 0)
                if i != 3:
                    next_halo = pltpu.roll(next_halo, 6 - 2 * i, 0)
                prev = jnp.where(row < 2, prev_halo, pltpu.roll(u[3], 2, 0))
                following = jnp.where(row >= 6, next_halo, pltpu.roll(u[0], 6, 0))
            elif direction == 1:
                prev, following = jumps_y(u[0], u[3])
            else:
                prev_halo = pltpu.roll(z_prev, 128 - k, 1) if k else z_prev
                next_halo = pltpu.roll(z_next, 127 - k, 1)
                prev = jnp.where(lane == 0, prev_halo, pltpu.roll(u[3], 1, 1))
                following = jnp.where(lane == 127, next_halo, pltpu.roll(u[0], 127, 1))
            d[0] = d[0] - 3.0 * (prev - u[0])
            d[3] = d[3] + 3.0 * (following - u[3])
            for end in range(4):
                g_ref[(direction * 4 + comp) * 64 + nodes[end]] = d[end]

    def pointwise(n, carry):
        v = [v_ref[c * 64 + n] for c in range(4)]
        g = [[g_ref[(d * 4 + c) * 64 + n] for c in range(4)] for d in range(3)]
        temperature = -1.0 / v[3]
        u = [v[i] * temperature for i in range(3)]
        scaled = VISCOSITY * temperature
        gu = [[scaled * (g[d][i] + u[i] * g[d][3]) for i in range(3)] for d in range(3)]
        third = (2.0 / 3.0) * (gu[0][0] + gu[1][1] + gu[2][2])
        conduct = FOURIER_LAW_ON * temperature * temperature
        tau = [[None] * 3 for _ in range(3)]
        for d in range(3):
            for i in range(d, 3):
                entry = gu[d][i] + gu[i][d]
                if i == d:
                    entry = entry - third
                tau[d][i] = entry
                tau[i][d] = entry
        for d in range(3):
            heat = u[0] * tau[d][0] + u[1] * tau[d][1] + u[2] * tau[d][2] + conduct * g[d][3]
            for c in range(3):
                f_ref[(d * 4 + c) * 64 + n] = tau[d][c]
            f_ref[(d * 4 + 3) * 64 + n] = heat
        return carry

    lax.fori_loop(0, 64, pointwise, 0, unroll=4)

    def face(direction, end):
        return lambda k: f_ref[(direction * 4 + k // 16) * 64 + line_nodes(direction, k % 16)[end]]

    pack_x(face(0, 0), face(0, 3), f1_ref, f2_ref)
    zup_ref[...], zlow_ref[...] = pack_z(face(2, 0), face(2, 3))


    for comp in range(4):
        for direction in range(3):
            for line in range(16):
                nodes = line_nodes(direction, line)
                u = [f_ref[(direction * 4 + comp) * 64 + n] for n in nodes]
                d = list(line_derivative(*u))
                if direction == 0:
                    prev = jnp.where(row < 2, 0.0, pltpu.roll(u[3], 2, 0))
                    following = jnp.where(row >= 6, 0.0, pltpu.roll(u[0], 6, 0))
                elif direction == 1:
                    prev, following = jumps_y(u[0], u[3])
                else:
                    prev = jnp.where(lane == 0, 0.0, pltpu.roll(u[3], 1, 1))
                    following = jnp.where(lane == 127, 0.0, pltpu.roll(u[0], 127, 1))
                d[0] = d[0] - 3.0 * (prev - u[0])
                d[3] = d[3] + 3.0 * (following - u[3])
                if direction == 1 and comp in (0, 2):
                    d[0] = d[0] + jnp.where(odd, 0.0, 6.0 * u[0])
                for end in range(4):
                    where = comp * 64 + nodes[end]
                    if direction == 0:
                        rate_ref[where] = d[end]
                    else:
                        rate_ref[where] = rate_ref[where] + d[end]


def rank_kernel(dest_ref, rank_ref, hot_ref, named_ref, count_ref):
    before = (iota((128, 128), 0) < iota((128, 128), 1)).astype(F32).astype(BF16)
    counter = jnp.concatenate([before, jnp.ones((128, 128), BF16)], axis=1)
    wall_ids = iota((N_WALL, 128), 0)
    low_ids = iota((256, 128), 0)
    blocks = M_DEV // 128
    for block in range(blocks):
        named = (wall_ids == dest_ref[0:1, 128 * block : 128 * block + 128]).astype(F32).astype(BF16)
        named_ref[pl.ds(N_WALL * block, N_WALL), :] = named
    count_ref[...] = jnp.dot(named_ref[...], counter, preferred_element_type=F32)
    total = jnp.zeros((N_WALL, 128), F32)
    for block in range(blocks):
        rows = pl.ds(N_WALL * block, N_WALL)
        lanes = pl.ds(128 * block, 128)
        own = wall_ids == dest_ref[0:1, 128 * block : 128 * block + 128]
        rank = jnp.sum(jnp.where(own, count_ref[rows, :128] + total, 0.0), axis=0, keepdims=True).astype(jnp.int32)
        rank_ref[pl.ds(block, 1), :] = rank
        hot_ref[:, lanes] = (low_ids == (rank & 255)).astype(F32).astype(BF16)
        total = total + count_ref[rows, 128:]


PROBE_BLOCK = 256


def probe_kernel(first, last, table_ref, elem_ref, coord_ref, probe_ref):
    points = gauss_points()
    width = PROBE_BLOCK
    scales = [float(1.0 / np.prod([points[i] - points[j] for j in range(4) if j != i])) for i in range(4)]

    def basis_rows(coordinate, index):
        if isinstance(index, int):
            product = scales[index]
            for other in range(4):
                if other != index:
                    product = product * (coordinate - float(points[other]))
            return product
        product = jnp.where(
            index == 0, scales[0], jnp.where(index == 1, scales[1], jnp.where(index == 2, scales[2], scales[3]))
        )
        for other in range(4):
            product = product * jnp.where(index == other, 1.0, coordinate - float(points[other]))
        return product

    low_ids = iota((256, width), 0)
    row16 = iota((16, width), 0)

    def probe_block(block, carry):
        here = pl.ds(pl.multiple_of(block * width, width), width)
        elem = elem_ref[0:1, here]
        hot = (low_ids == elem & 255).astype(F32).astype(BF16)
        picked = jnp.dot(table_ref[...], hot, preferred_element_type=F32).reshape(4, 2, 24, 8, width)
        group = jnp.broadcast_to(elem >> 8, (8, width))
        both = picked[:, 0] + picked[:, 1]
        values = both[0]
        for g in range(1, 4):
            values = jnp.where((group == g)[None], both[g], values)
        values = values.reshape(192, width)
        coords = [(2.0 * coord_ref[d : d + 1, here].astype(F32) + 1.0) / RES - 1.0 for d in range(3)]
        wide = [jnp.broadcast_to(coords[d], (16, width)) for d in range(3)]
        along_yz = basis_rows(wide[1], row16 // 4) * basis_rows(wide[2], row16 % 4)
        along_x = [basis_rows(wide[0], a) for a in range(4)]
        results = []
        for field in range(3):
            total = None
            for a in range(4):
                term = along_x[a] * values[64 * field + 16 * a : 64 * field + 16 * a + 16]
                total = term if total is None else total + term
            results.append(jnp.sum(total * along_yz, axis=0, keepdims=True))
        layer = (elem // EZ % EY).astype(F32)
        results.append(2.0 * layer + 1.0 + coords[1])
        for field in range(4):
            for i in range(width // 128):
                probe_ref[field, pl.ds((block - first) * (width // 128) + i, 1), :] = results[field][
                    :, 128 * i : 128 * (i + 1)
                ]
        return carry

    lax.fori_loop(first, last, probe_block, 0, unroll=4)


SEND_BLOCK = 1024
PER = CAP // 128
CHUNK = 4 * PER + 4


def send_kernel(*refs):
    n_probe = len(refs) - 9
    probe_refs = refs[:n_probe]
    rank_ref, dest_ref, hot_ref, rough_ref, zup_ref, zlow_ref, send_ref, own_ref, lhs_ref = refs[n_probe:]
    rows = M_DEV // 128
    rho, mx, mz, height = [jnp.concatenate([ref[f] for ref in probe_refs], axis=0) for f in range(4)]
    inv_rho = 1.0 / rho
    vel_x = mx * inv_rho
    vel_z = mz * inv_rho
    slip = jnp.maximum(jnp.sqrt(vel_x * vel_x + vel_z * vel_z), 0.5)
    values = [slip * mx, slip * mz, height * slip * rho * (1.0 / VISCOSITY)]
    parts = []
    for f in range(3):
        own_ref[f] = values[f]
        high = values[f].astype(BF16).astype(F32)
        parts += [high, values[f] - high]

    code = (rank_ref[...] // 256) * N_WALL + dest_ref[...]
    code_ids = iota((96, 128), 0)
    total = jnp.zeros((576, 256), F32)
    per = SEND_BLOCK // 128
    for block in range(M_DEV // SEND_BLOCK):
        for i in range(per):
            r = block * per + i
            match = code_ids == code[r : r + 1]
            for part in range(6):
                lhs_ref[pl.ds(96 * part, 96), pl.ds(128 * r, 128)] = jnp.where(
                    match, parts[part][r : r + 1], 0.0
                ).astype(BF16)
        span = pl.ds(block * SEND_BLOCK, SEND_BLOCK)
        total = total + lax.dot_general(
            lhs_ref[:, span], hot_ref[:, span], (((1,), (1,)), ((), ())), preferred_element_type=F32
        )
    for chunk in range(PER):
        q, half = chunk // 2, chunk % 2
        lanes = slice(128 * half, 128 * half + 128)
        for w in range(0, N_WALL, 8):
            for f in range(3):
                base = 192 * f + q * N_WALL + w
                send_ref[pl.ds(w * CHUNK + f * PER + chunk, 8, stride=CHUNK), :] = (
                    total[base : base + 8, lanes] + total[base + 96 : base + 104, lanes]
                )
            send_ref[pl.ds(w * CHUNK + 3 * PER + chunk, 8, stride=CHUNK), :] = rough_ref[
                pl.ds(w * PER + chunk, 8, stride=PER), :
            ]


    half = iota((4, 128), 1) < 64
    upper, lower = [
        jnp.where(half, ref[0:4, :], pltpu.roll(ref[...], 64, 1)[4:8]) for ref in (zup_ref, zlow_ref)
    ]
    target = lax.rem(lax.axis_index("wall") + 1, N_WALL)
    for w in range(N_WALL):
        send_ref[pl.ds(w * CHUNK + 4 * PER, 4), :] = jnp.where(target == w, upper, lower)


def shear_scale(log_term):
    ratio = jnp.ones_like(log_term)
    for sweep in range(NEWTON):
        numerator = KARMAN * ratio - log_term + jnp.log(ratio)
        ratio = ratio - RELAXATION * ratio * numerator / (KARMAN * ratio + 1.0)
    return 1.0 / (ratio * ratio)


def final_kernel(part_ref, x1_ref, x2_ref, got_ref, own_ref, rank_ref, dest_ref, rough_ref,
                 rate_ref, wall_ref, table_ref, factor_ref, shear_ref, out_ref, sems):
    row = iota((8, 128), 0)
    lane = iota((8, 128), 1)
    here = lax.axis_index("wall")
    z_halo = []
    for source in (here + N_WALL - 1, here + 1):
        start = pl.multiple_of(lax.rem(source, N_WALL) * CHUNK + 4 * PER - 4, 8)
        folded = got_ref[pl.ds(start, 8), :]
        unfolded = pltpu.roll(folded, 64, 1)
        z_halo.append(jnp.concatenate([folded[4:8], unfolded[4:8]], axis=0))

    for chunk in range(PER):
        for w in range(0, N_WALL, 16):
            value = jnp.concatenate(
                [got_ref[pl.ds((w + 8 * i) * CHUNK + 3 * PER + chunk, 8, stride=CHUNK), :] for i in range(2)], axis=0
            )
            high = value.astype(BF16)
            table_ref[pl.ds(chunk * N_WALL + w, 16), :128] = high
            table_ref[pl.ds(chunk * N_WALL + w, 16), 128:] = (value - high.astype(F32)).astype(BF16)
    code = (rank_ref[...] >> 7) * N_WALL + dest_ref[...]
    place = rank_ref[...] & 127
    code_ids = iota((PER * N_WALL, 128), 0)
    ids = iota((128, 128), 0)
    for block in range(M_DEV // 512):
        hot = jnp.concatenate(
            [jnp.where(ids == place[r : r + 1], 1.0, 0.0).astype(BF16) for r in range(4 * block, 4 * block + 4)], axis=1
        )
        found = jnp.dot(table_ref[...], jnp.concatenate([hot, hot], axis=0), preferred_element_type=F32)
        for i in range(4):
            r = 4 * block + i
            picked = jnp.where(code_ids == code[r : r + 1], found[:, 128 * i : 128 * i + 128], 0.0)
            factor_ref[pl.ds(r, 1), :] = jnp.sum(picked, axis=0, keepdims=True)
    scale = shear_scale(jnp.log(factor_ref[...] * own_ref[2]))
    shear_ref[...] = jnp.zeros_like(shear_ref)
    for comp in range(2):
        shear = own_ref[comp] * scale
        for pair in range(16):
            shear_ref[pl.ds(128 * comp + 8 * pair, 4, stride=2), :] = shear[4 * pair : 4 * pair + 4]

    for chunk in range(PER):
        for w in range(0, N_WALL, 8):
            vx, vz, reynolds = [
                got_ref[pl.ds(w * CHUNK + f * PER + chunk, 8, stride=CHUNK), :] for f in range(3)
            ]
            used = reynolds > 0.0
            factor = rough_ref[pl.ds(w * PER + chunk, 8, stride=PER), :]
            scale = shear_scale(jnp.log(factor * jnp.where(used, reynolds, 1.0)))
            place = w * PER * 2 + chunk * 2
            wall_ref[pl.ds(place, 8, stride=2 * PER), :] = jnp.where(used, vx * scale, 0.0)
            wall_ref[pl.ds(place + 1, 8, stride=2 * PER), :] = jnp.where(used, vz * scale, 0.0)

    copies = []
    for n in range(64):
        a, b, c = n // 16, n // 4 % 4, n % 4
        for comp in range(4):
            total = part_ref[comp * 64 + n]
            if a in (0, 3):
                k = comp * 16 + 4 * b + c
                i = k % 4
                halo = x_halos(x1_ref, x2_ref, k // 4)[0 if a == 0 else 1]
                shift = (8 - 2 * i) % 8 if a == 0 else 6 - 2 * i
                if shift:
                    halo = pltpu.roll(halo, shift, 0)
                if a == 0:
                    total = total - jnp.where(row < 2, 3.0 * halo, 0.0)
                else:
                    total = total + jnp.where(row >= 6, 3.0 * halo, 0.0)
            if c in (0, 3):
                k = comp * 16 + 4 * a + b
                halo = z_halo[0 if c == 0 else 1]
                shift = (128 - k) % 128 if c == 0 else 127 - k
                if shift:
                    halo = pltpu.roll(halo, shift, 1)
                if c == 0:
                    total = total - jnp.where(lane == 0, 3.0 * halo, 0.0)
                else:
                    total = total + jnp.where(lane == 127, 3.0 * halo, 0.0)
            if b == 0 and comp in (0, 2):
                total = total - 6.0 * shear_ref[pl.ds((comp // 2) * 128 + (4 * a + c) * 8, 8), :]
            out_ref[pl.ds(n * 32 + comp, 8, stride=4), :] = total
        if n % 16 == 15:
            span = pl.ds(512 * a, 512)
            copies.append(pltpu.make_async_copy(out_ref.at[span], rate_ref.at[span], sems.at[a]))
            copies[-1].start()
    for copy in copies:
        copy.wait()


VMEM = pl.BlockSpec(memory_space=pltpu.VMEM)
HBM = pl.BlockSpec(memory_space=pltpu.HBM)


def call(kernel, inputs, outputs, scratch=(), name=None, cost=1, specs=None, out_specs=None, limit=8):
    return pl.pallas_call(
        kernel,
        out_shape=[jax.ShapeDtypeStruct(shape, dtype) for shape, dtype in outputs],
        in_specs=specs or [VMEM] * len(inputs),
        out_specs=out_specs or [VMEM] * len(outputs),
        scratch_shapes=[s if not isinstance(s, tuple) else pltpu.VMEM(*s) for s in scratch],
        name=name,
        cost_estimate=pl.CostEstimate(flops=cost * 10**9, bytes_accessed=cost * 3 * 10**6, transcendentals=0),
        compiler_params=pltpu.CompilerParams(vmem_limit_bytes=int(limit * 1024 * 1024)),
    )(*inputs)


def exchange(axis, first, second, stage):
    count = lax.axis_size(axis)
    with jax.named_scope(stage + "_first"):
        one = lax.ppermute(first, axis, [(i, i + 1 - 2 * (i % 2)) for i in range(count)])
    with jax.named_scope(stage + "_second"):
        other = lax.ppermute(second, axis, [(i, (i - 1 + 2 * (i % 2)) % count) for i in range(count)])
    return one, other


def after(value, *others):
    return lax.optimization_barrier((value, *others))[0]


CUTS = (0, 8, 20, 32)
ENTROPY_LIMIT = 52


def local(flow_state, match_elem, match_coord, match_dest, roughness):
    faces = [((128, 128), F32), ((128, 128), F32), ((8, 128), F32), ((8, 128), F32)]
    nodal = ((256, 8, 128), F32)
    flow_rows = flow_state.transpose(1, 0, 2).reshape(5, 8, 8, 8, 128).transpose(0, 1, 3, 2, 4).reshape(5, 512, 128)
    dest = match_dest.reshape(64, 128)
    elem = match_elem.reshape(1, M_DEV)
    rough = roughness.reshape(N_WALL * PER, 128)
    v, table, x1, x2, z1, z2 = call(
        entropy_kernel,
        [flow_rows],
        [nodal, ((1536, 256), BF16)] + faces,
        [((5, 512, 128), F32), pltpu.SemaphoreType.DMA((4,))],
        name="entropy",
        specs=[HBM],
        limit=ENTROPY_LIMIT,
    )
    rank, hot = call(
        rank_kernel,
        [match_dest.reshape(1, M_DEV)],
        [((64, 128), jnp.int32), ((256, M_DEV), BF16)],
        [((2048, 128), BF16), ((2048, 256), F32)],
        name="rank",
    )
    probes = []
    for i, (first, last) in enumerate(zip(CUTS[:-1], CUTS[1:])):
        (probe,) = call(
            lambda *refs, first=first, last=last: probe_kernel(first, last, *refs),
            [after(table, probes[-1]) if probes else after(table, rank), elem, match_coord],
            [((4, (last - first) * PROBE_BLOCK // 128, 128), F32)],
            name=f"probe{i}",
            cost=5,
        )
        probes.append(probe)
    halos = [*exchange("slab", x1, after(x2, rank), "vx")]
    halos += exchange("wall", after(z1, probes[0]), after(z2, probes[1]), "vz")
    part, f1, f2, zup, zlow = call(
        flux_kernel,
        [after(v, probes[-1]), *halos],
        [nodal] + faces,
        [((768, 8, 128), F32), ((768, 8, 128), F32)],
        name="flux",
        limit=12,
    )
    send, own = call(
        send_kernel,
        [*probes, after(rank, f1), dest, hot, rough, zup, zlow],
        [((N_WALL * CHUNK, 128), F32), ((3, 64, 128), F32)],
        [((576, M_DEV), BF16)],
        name="send",
        cost=3,
        limit=16,
    )
    got = lax.all_to_all(send.reshape(N_WALL, 1, CHUNK * 128), "wall", 0, 0, tiled=True)
    halos = exchange("slab", f1, after(f2, send), "fx")
    rate, wall = call(
        final_kernel,
        [part, *halos, got.reshape(N_WALL * CHUNK, 128), own, rank, dest, rough],
        [((2048, 128), F32), ((2 * N_WALL * PER, 128), F32)],
        [
            ((PER * N_WALL, 256), BF16),
            ((64, 128), F32),
            ((256, 128), F32),
            ((2048, 128), F32),
            pltpu.SemaphoreType.DMA((4,)),
        ],
        name="final",
        out_specs=[HBM, VMEM],
    )
    rate = rate.reshape(64, 8, 4, 128).transpose(0, 2, 1, 3).reshape(64, 4, 1024)
    wall_shear = wall.reshape(N_WALL * PER, 2, 128).transpose(1, 0, 2).reshape(2, N_WALL * CAP)
    return (rate, wall_shear)


def solution(mesh):
    return jax.shard_map(
        local,
        mesh=mesh,
        in_specs=(
            P(None, None, ("slab", "wall")),
            P(("slab", "wall")),
            P(None, ("slab", "wall")),
            P(("slab", "wall"), None),
            P(("slab", "wall")),
        ),
        out_specs=(P(None, None, ("slab", "wall")), P(None, ("slab", "wall"))),
        check_vma=False,
    )
```

```python
import jax
import jax.numpy as jnp
import numpy as np
from jax import lax
from jax.experimental import pallas as pl
from jax.experimental.pallas import tpu as pltpu
from jax.sharding import PartitionSpec as P

EX = 4
EY = 2
EZ = 128
RES = 16
NEWTON = 8
CAP = 640
N_WALL = 32
M_DEV = 8192

VISCOSITY = 0.05
FOURIER_LAW_ON = 0.07 / 0.288
KARMAN = 0.41
RELAXATION = 0.35
F32 = jnp.float32
BF16 = jnp.bfloat16


def gauss_points():
    return np.array([-1.0, -1.0 / np.sqrt(5.0), 1.0 / np.sqrt(5.0), 1.0])


def derivative_matrix():
    points = gauss_points()
    bary = [
        1.0 / np.prod([points[i] - points[j] for j in range(4) if j != i]) for i in range(4)
    ]
    matrix = np.zeros((4, 4))
    for i in range(4):
        for j in range(4):
            if i != j:
                matrix[i, j] = bary[j] / bary[i] / (points[i] - points[j])
        matrix[i, i] = -np.sum(matrix[i])
    return matrix


D = derivative_matrix()
EVEN0 = float(0.5 * (D[0, 0] + D[0, 3]))
EVEN1 = float(0.5 * (D[1, 0] + D[1, 3]))
ODD00 = float(0.5 * (D[0, 0] - D[0, 3]))
ODD01 = float(0.5 * (D[0, 1] - D[0, 2]))
ODD10 = float(0.5 * (D[1, 0] - D[1, 3]))
ODD11 = float(0.5 * (D[1, 1] - D[1, 2]))


def line_derivative(u0, u1, u2, u3):
    even = (u0 + u3) - (u1 + u2)
    odd0 = u0 - u3
    odd1 = u1 - u2
    half0 = EVEN0 * even
    half1 = EVEN1 * even
    mean0 = ODD00 * odd0 + ODD01 * odd1
    mean1 = ODD10 * odd0 + ODD11 * odd1
    return mean0 + half0, mean1 + half1, mean1 - half1, mean0 - half0


def iota(shape, dim):
    return lax.broadcasted_iota(jnp.int32, shape, dim)


def entropy_of(rho, mx, my, mz, energy):
    inv_rho = 1.0 / rho
    speed_sq = mx * mx + my * my + mz * mz
    pressure = 0.4 * (energy - 0.5 * speed_sq * inv_rho)
    entropy_s = jnp.log(pressure) - 1.4 * jnp.log(rho)
    inv_p = 1.0 / pressure
    leading = (1.4 - entropy_s) / 0.4 - 0.5 * speed_sq * inv_rho * inv_p
    return leading, mx * inv_p, my * inv_p, mz * inv_p, -rho * inv_p


def line_nodes(direction, line):
    outer, inner = line // 4, line % 4
    if direction == 0:
        return [16 * a + 4 * outer + inner for a in range(4)]
    if direction == 1:
        return [16 * outer + 4 * b + inner for b in range(4)]
    return [16 * outer + 4 * inner + c for c in range(4)]


def is_even(axis):
    return lax.rem(lax.axis_index(axis), 2) == 0


def pick(condition, one, other):
    return lax.select(jnp.broadcast_to(condition, one.shape), one, other)


def pack_x(get_lower, get_upper, first_ref, second_ref):
    even = is_even("slab")
    pair = iota((8, 128), 0) // 2
    for block in range(16):
        upper = pltpu.roll(get_upper(4 * block), 2, 0)
        lower = get_lower(4 * block)
        for i in range(1, 4):
            upper = jnp.where(pair == i, pltpu.roll(get_upper(4 * block + i), (2 + 2 * i) % 8, 0), upper)
            lower = jnp.where(pair == i, pltpu.roll(get_lower(4 * block + i), 2 * i, 0), lower)
        first_ref[pl.ds(8 * block, 8), :] = pick(even, upper, lower)
        second_ref[pl.ds(8 * block, 8), :] = pick(even, lower, upper)


def pack_z(get_lower, get_upper):
    lane = iota((8, 128), 1)
    upper = jnp.zeros((8, 128), F32)
    lower = jnp.zeros((8, 128), F32)
    for k in range(64):
        upper = jnp.where(lane == k, pltpu.roll(get_upper(k), (k + 1) % 128, 1), upper)
        low = get_lower(k)
        lower = jnp.where(lane == k, low if k == 0 else pltpu.roll(low, k, 1), lower)
    return upper, lower


def x_halos(first_ref, second_ref, block):
    even = is_even("slab")
    first = first_ref[pl.ds(8 * block, 8), :]
    second = second_ref[pl.ds(8 * block, 8), :]
    return pick(even, second, first), pick(even, first, second)


def join_x(u, halos, i, row):
    prev_halo, next_halo = halos
    if i:
        prev_halo = pltpu.roll(prev_halo, 8 - 2 * i, 0)
    if i != 3:
        next_halo = pltpu.roll(next_halo, 6 - 2 * i, 0)
    prev = jnp.where(row < 2, prev_halo, pltpu.roll(u[3], 2, 0))
    following = jnp.where(row >= 6, next_halo, pltpu.roll(u[0], 6, 0))
    return prev, following


def entropy_kernel(flow_ref, v_ref, table_ref, x1_ref, x2_ref, z1_ref, z2_ref, rows_ref, sems):
    copies = [
        pltpu.make_async_copy(
            flow_ref.at[:, pl.ds(128 * part, 128), :], rows_ref.at[:, pl.ds(128 * part, 128), :], sems.at[part]
        )
        for part in range(4)
    ]
    for copy in copies:
        copy.start()
    for part in range(4):
        copies[part].wait()
        for n in range(16 * part, 16 * part + 16):
            start = n // 8 * 64 + n % 8
            values = entropy_of(*[rows_ref[c, pl.ds(start, 8, stride=8), :] for c in range(5)])
            for k in range(4):
                v_ref[k * 64 + n] = values[1 + k]
        for field, c in enumerate((0, 1, 3)):
            for j in range(8):
                value = jnp.concatenate(
                    [rows_ref[c, pl.ds(part * 128 + half * 64 + j * 8, 8), :] for half in range(2)], axis=0
                )
                high = value.astype(BF16)
                low = (value - high.astype(F32)).astype(BF16)
                base = j // 2 * 384 + field * 64 + part * 16
                lanes = pl.ds(j % 2 * 128, 128)
                table_ref[pl.ds(base, 16), lanes] = high
                table_ref[pl.ds(base + 192, 16), lanes] = low

    def face(direction, end):
        return lambda k: v_ref[(k // 16) * 64 + line_nodes(direction, k % 16)[end]]

    pack_x(face(0, 0), face(0, 3), x1_ref, x2_ref)
    upper, lower = pack_z(face(2, 0), face(2, 3))
    even = is_even("wall")
    z1_ref[...] = pick(even, upper, lower)
    z2_ref[...] = pick(even, lower, upper)


def jumps_y(lower, upper):
    odd = iota((8, 128), 0) % 2 == 1
    prev = jnp.where(odd, pltpu.roll(upper, 1, 0), lower)
    following = jnp.where(odd, upper, pltpu.roll(lower, 7, 0))
    return prev, following


FLUX = ((0, 1, 2, 6), (1, 3, 4, 7), (2, 4, 5, 8))


def flux_kernel(v_ref, x1_ref, x2_ref, z1_ref, z2_ref,
                rate_ref, fx1_ref, fx2_ref, fz1_ref, fz2_ref, g_ref, f_ref):
    row = iota((8, 128), 0)
    lane = iota((8, 128), 1)
    odd = row % 2 == 1
    even = is_even("wall")
    z_prev = pick(even, z2_ref[...], z1_ref[...])
    z_next = pick(even, z1_ref[...], z2_ref[...])

    for k in range(64):
        comp, line = k // 16, k % 16
        for direction in range(3):
            nodes = line_nodes(direction, line)
            u = [v_ref[comp * 64 + n] for n in nodes]
            d = list(line_derivative(*u))
            if direction == 0:
                prev, following = join_x(u, x_halos(x1_ref, x2_ref, k // 4), k % 4, row)
            elif direction == 1:
                prev, following = jumps_y(u[0], u[3])
            else:
                prev_halo = pltpu.roll(z_prev, 128 - k, 1) if k else z_prev
                next_halo = pltpu.roll(z_next, 127 - k, 1)
                prev = jnp.where(lane == 0, prev_halo, pltpu.roll(u[3], 1, 1))
                following = jnp.where(lane == 127, next_halo, pltpu.roll(u[0], 127, 1))
            d[0] = d[0] - 3.0 * (prev - u[0])
            d[3] = d[3] + 3.0 * (following - u[3])
            for end in range(4):
                g_ref[(direction * 4 + comp) * 64 + nodes[end]] = d[end]

    def pointwise(n, carry):
        v = [v_ref[c * 64 + n] for c in range(4)]
        g = [[g_ref[(d * 4 + c) * 64 + n] for c in range(4)] for d in range(3)]
        temperature = -1.0 / v[3]
        u = [v[i] * temperature for i in range(3)]
        scaled = VISCOSITY * temperature
        gu = [[scaled * (g[d][i] + u[i] * g[d][3]) for i in range(3)] for d in range(3)]
        third = (2.0 / 3.0) * (gu[0][0] + gu[1][1] + gu[2][2])
        conduct = FOURIER_LAW_ON * temperature * temperature
        tau = [[None] * 3 for _ in range(3)]
        for d in range(3):
            for i in range(d, 3):
                entry = gu[d][i] + gu[i][d]
                if i == d:
                    entry = entry - third
                tau[d][i] = entry
                tau[i][d] = entry
        for d in range(3):
            heat = u[0] * tau[d][0] + u[1] * tau[d][1] + u[2] * tau[d][2] + conduct * g[d][3]
            for c in range(d, 3):
                f_ref[FLUX[d][c] * 64 + n] = tau[d][c]
            f_ref[FLUX[d][3] * 64 + n] = heat
        return carry

    lax.fori_loop(0, 64, pointwise, 0, unroll=4)

    def face(direction, end):
        return lambda k: f_ref[FLUX[direction][k // 16] * 64 + line_nodes(direction, k % 16)[end]]

    pack_x(face(0, 0), face(0, 3), fx1_ref, fx2_ref)
    upper, lower = pack_z(face(2, 0), face(2, 3))
    fz1_ref[...] = pick(even, upper, lower)
    fz2_ref[...] = pick(even, lower, upper)

    for comp in range(4):
        for direction in range(3):
            for line in range(16):
                nodes = line_nodes(direction, line)
                u = [f_ref[FLUX[direction][comp] * 64 + n] for n in nodes]
                d = list(line_derivative(*u))
                if direction == 0:
                    prev = jnp.where(row < 2, 0.0, pltpu.roll(u[3], 2, 0))
                    following = jnp.where(row >= 6, 0.0, pltpu.roll(u[0], 6, 0))
                elif direction == 1:
                    prev, following = jumps_y(u[0], u[3])
                else:
                    prev = jnp.where(lane == 0, 0.0, pltpu.roll(u[3], 1, 1))
                    following = jnp.where(lane == 127, 0.0, pltpu.roll(u[0], 127, 1))
                d[0] = d[0] - 3.0 * (prev - u[0])
                d[3] = d[3] + 3.0 * (following - u[3])
                if direction == 1 and comp in (0, 2):
                    d[0] = d[0] + jnp.where(odd, 0.0, 6.0 * u[0])
                for end in range(4):
                    where = comp * 64 + nodes[end]
                    if direction == 0:
                        rate_ref[where] = d[end]
                    else:
                        rate_ref[where] = rate_ref[where] + d[end]


def assemble_kernel(part_ref, x1_ref, x2_ref, z1_ref, z2_ref, rate_ref, bottom_ref, out_ref, sems):
    row = iota((8, 128), 0)
    lane = iota((8, 128), 1)
    even = is_even("wall")
    z_prev = pick(even, z2_ref[...], z1_ref[...])
    z_next = pick(even, z1_ref[...], z2_ref[...])
    copies = []
    for n in range(64):
        a, b, c = n // 16, n // 4 % 4, n % 4
        for comp in range(4):
            total = part_ref[comp * 64 + n]
            if a in (0, 3):
                k = comp * 16 + 4 * b + c
                i = k % 4
                halo = x_halos(x1_ref, x2_ref, k // 4)[0 if a == 0 else 1]
                shift = (8 - 2 * i) % 8 if a == 0 else 6 - 2 * i
                if shift:
                    halo = pltpu.roll(halo, shift, 0)
                if a == 0:
                    total = total - jnp.where(row < 2, 3.0 * halo, 0.0)
                else:
                    total = total + jnp.where(row >= 6, 3.0 * halo, 0.0)
            if c in (0, 3):
                k = comp * 16 + 4 * a + b
                halo = z_prev if c == 0 else z_next
                shift = (128 - k) % 128 if c == 0 else 127 - k
                if shift:
                    halo = pltpu.roll(halo, shift, 1)
                if c == 0:
                    total = total - jnp.where(lane == 0, 3.0 * halo, 0.0)
                else:
                    total = total + jnp.where(lane == 127, 3.0 * halo, 0.0)
            if b == 0:
                bottom_ref[(4 * a + c) * 4 + comp] = total
            else:
                out_ref[pl.ds(n * 32 + comp, 8, stride=4), :] = total
        if n % 16 == 15:
            span = pl.ds(512 * a + 128, 384)
            copies.append(pltpu.make_async_copy(out_ref.at[span], rate_ref.at[span], sems.at[a]))
            copies[-1].start()
    for copy in copies:
        copy.wait()


def rank_kernel(dest_ref, rank_ref, hot_ref, named_ref, count_ref):
    before = (iota((128, 128), 0) < iota((128, 128), 1)).astype(F32).astype(BF16)
    counter = jnp.concatenate([before, jnp.ones((128, 128), BF16)], axis=1)
    wall_ids = iota((N_WALL, 128), 0)
    low_ids = iota((256, 128), 0).astype(jnp.int16)
    one, zero = jnp.ones((), BF16), jnp.zeros((), BF16)
    blocks = M_DEV // 128
    for block in range(blocks):
        named = (wall_ids == dest_ref[0:1, 128 * block : 128 * block + 128]).astype(F32).astype(BF16)
        named_ref[pl.ds(N_WALL * block, N_WALL), :] = named
    count_ref[...] = jnp.dot(named_ref[...], counter, preferred_element_type=F32)
    total = jnp.zeros((N_WALL, 128), F32)
    for block in range(blocks):
        rows = pl.ds(N_WALL * block, N_WALL)
        lanes = pl.ds(128 * block, 128)
        own = wall_ids == dest_ref[0:1, 128 * block : 128 * block + 128]
        rank = jnp.sum(jnp.where(own, count_ref[rows, :128] + total, 0.0), axis=0, keepdims=True).astype(jnp.int32)
        rank_ref[pl.ds(block, 1), :] = rank
        low = jnp.broadcast_to(rank & 255, (256, 128)).astype(jnp.int16)
        hot_ref[:, lanes] = jnp.where(low_ids == low, one, zero)
        total = total + count_ref[rows, 128:]


PROBE_BLOCK = 256


def probe_kernel(first, last, table_ref, elem_ref, coord_ref, probe_ref):
    points = gauss_points()
    width = PROBE_BLOCK
    scales = [float(1.0 / np.prod([points[i] - points[j] for j in range(4) if j != i])) for i in range(4)]

    def basis_rows(coordinate, index):
        if isinstance(index, int):
            product = scales[index]
            for other in range(4):
                if other != index:
                    product = product * (coordinate - float(points[other]))
            return product
        product = jnp.where(
            index == 0, scales[0], jnp.where(index == 1, scales[1], jnp.where(index == 2, scales[2], scales[3]))
        )
        for other in range(4):
            product = product * jnp.where(index == other, 1.0, coordinate - float(points[other]))
        return product

    low_ids = iota((256, width), 0)
    row16 = iota((16, width), 0)

    def probe_block(block, carry):
        here = pl.ds(pl.multiple_of(block * width, width), width)
        elem = elem_ref[0:1, here]
        hot = (low_ids == elem & 255).astype(F32).astype(BF16)
        picked = jnp.dot(table_ref[...], hot, preferred_element_type=F32).reshape(4, 2, 24, 8, width)
        group = jnp.broadcast_to(elem >> 8, (8, width))
        both = picked[:, 0] + picked[:, 1]
        values = both[0]
        for g in range(1, 4):
            values = jnp.where((group == g)[None], both[g], values)
        values = values.reshape(192, width)
        coords = [(2.0 * coord_ref[d : d + 1, here].astype(F32) + 1.0) / RES - 1.0 for d in range(3)]
        wide = [jnp.broadcast_to(coords[d], (16, width)) for d in range(3)]
        along_yz = basis_rows(wide[1], row16 // 4) * basis_rows(wide[2], row16 % 4)
        along_x = [basis_rows(wide[0], a) for a in range(4)]
        results = []
        for field in range(3):
            total = None
            for a in range(4):
                term = along_x[a] * values[64 * field + 16 * a : 64 * field + 16 * a + 16]
                total = term if total is None else total + term
            results.append(jnp.sum(total * along_yz, axis=0, keepdims=True))
        layer = (elem // EZ % EY).astype(F32)
        results.append(2.0 * layer + 1.0 + coords[1])
        for field in range(4):
            for i in range(width // 128):
                probe_ref[field, pl.ds((block - first) * (width // 128) + i, 1), :] = results[field][
                    :, 128 * i : 128 * (i + 1)
                ]
        return carry

    lax.fori_loop(first, last, probe_block, 0, unroll=4)


SEND_BLOCK = 1024
PER = CAP // 128
CHUNK = 4 * PER


def send_kernel(*refs):
    n_probe = len(refs) - 7
    probe_refs = refs[:n_probe]
    rank_ref, dest_ref, hot_ref, rough_ref, send_ref, own_ref, lhs_ref = refs[n_probe:]
    rows = M_DEV // 128
    rho, mx, mz, height = [jnp.concatenate([ref[f] for ref in probe_refs], axis=0) for f in range(4)]
    inv_rho = 1.0 / rho
    vel_x = mx * inv_rho
    vel_z = mz * inv_rho
    slip = jnp.maximum(jnp.sqrt(vel_x * vel_x + vel_z * vel_z), 0.5)
    values = [slip * mx, slip * mz, height * slip * rho * (1.0 / VISCOSITY)]
    parts = []
    for f in range(3):
        own_ref[f] = values[f]
        high = values[f].astype(BF16).astype(F32)
        parts += [high, values[f] - high]

    code = (rank_ref[...] // 256) * N_WALL + dest_ref[...]
    code_ids = iota((96, 128), 0)
    total = jnp.zeros((576, 256), F32)
    per = SEND_BLOCK // 128
    for block in range(M_DEV // SEND_BLOCK):
        for i in range(per):
            r = block * per + i
            match = code_ids == code[r : r + 1]
            for part in range(6):
                lhs_ref[pl.ds(96 * part, 96), pl.ds(128 * r, 128)] = jnp.where(
                    match, parts[part][r : r + 1], 0.0
                ).astype(BF16)
        span = pl.ds(block * SEND_BLOCK, SEND_BLOCK)
        total = total + lax.dot_general(
            lhs_ref[:, span], hot_ref[:, span], (((1,), (1,)), ((), ())), preferred_element_type=F32
        )
    for chunk in range(PER):
        q, half = chunk // 2, chunk % 2
        lanes = slice(128 * half, 128 * half + 128)
        for w in range(0, N_WALL, 8):
            for f in range(3):
                base = 192 * f + q * N_WALL + w
                send_ref[pl.ds(w * CHUNK + f * PER + chunk, 8, stride=CHUNK), :] = (
                    total[base : base + 8, lanes] + total[base + 96 : base + 104, lanes]
                )
            send_ref[pl.ds(w * CHUNK + 3 * PER + chunk, 8, stride=CHUNK), :] = rough_ref[
                pl.ds(w * PER + chunk, 8, stride=PER), :
            ]


def shear_scale(log_term):
    ratio = jnp.ones_like(log_term)
    for sweep in range(NEWTON):
        numerator = KARMAN * ratio - log_term + jnp.log(ratio)
        ratio = ratio - RELAXATION * ratio * numerator / (KARMAN * ratio + 1.0)
    return 1.0 / (ratio * ratio)


def final_kernel(kept_ref, bottom_ref, got_ref, own_ref, rank_ref, dest_ref, rough_ref,
                 rate_ref, wall_ref, table_ref, factor_ref, shear_ref, out_ref, sems):
    for chunk in range(PER):
        for w in range(0, N_WALL, 16):
            value = jnp.concatenate(
                [got_ref[pl.ds((w + 8 * i) * CHUNK + 3 * PER + chunk, 8, stride=CHUNK), :] for i in range(2)], axis=0
            )
            high = value.astype(BF16)
            table_ref[pl.ds(chunk * N_WALL + w, 16), :128] = high
            table_ref[pl.ds(chunk * N_WALL + w, 16), 128:] = (value - high.astype(F32)).astype(BF16)
    code = (rank_ref[...] >> 7) * N_WALL + dest_ref[...]
    code_ids = iota((PER * N_WALL, 128), 0)
    ids = iota((128, 512), 0).astype(jnp.int16)
    one, zero = jnp.ones((), BF16), jnp.zeros((), BF16)
    for block in range(M_DEV // 512):
        place = jnp.concatenate([rank_ref[r : r + 1, :] & 127 for r in range(4 * block, 4 * block + 4)], axis=1)
        hot = jnp.where(ids == jnp.broadcast_to(place, (128, 512)).astype(jnp.int16), one, zero)
        found = jnp.dot(table_ref[...], jnp.concatenate([hot, hot], axis=0), preferred_element_type=F32)
        for i in range(4):
            r = 4 * block + i
            picked = jnp.where(code_ids == code[r : r + 1], found[:, 128 * i : 128 * i + 128], 0.0)
            factor_ref[pl.ds(r, 1), :] = jnp.sum(picked, axis=0, keepdims=True)
    scale = shear_scale(jnp.log(factor_ref[...] * own_ref[2]))
    shear_ref[...] = jnp.zeros_like(shear_ref)
    for comp in range(2):
        shear = own_ref[comp] * scale
        for pair in range(16):
            shear_ref[pl.ds(128 * comp + 8 * pair, 4, stride=2), :] = shear[4 * pair : 4 * pair + 4]
    copies = []
    for a in range(4):
        for c in range(4):
            for comp in range(4):
                total = bottom_ref[(4 * a + c) * 4 + comp]
                if comp in (0, 2):
                    total = total - 6.0 * shear_ref[pl.ds((comp // 2) * 128 + (4 * a + c) * 8, 8), :]
                out_ref[pl.ds(128 * a + 32 * c + comp, 8, stride=4), :] = total
        copies.append(
            pltpu.make_async_copy(out_ref.at[pl.ds(128 * a, 128)], rate_ref.at[pl.ds(512 * a, 128)], sems.at[a])
        )
        copies[-1].start()

    for chunk in range(PER):
        for w in range(0, N_WALL, 8):
            vx, vz, reynolds = [
                got_ref[pl.ds(w * CHUNK + f * PER + chunk, 8, stride=CHUNK), :] for f in range(3)
            ]
            used = reynolds > 0.0
            factor = rough_ref[pl.ds(w * PER + chunk, 8, stride=PER), :]
            scale = shear_scale(jnp.log(factor * jnp.where(used, reynolds, 1.0)))
            place = w * PER * 2 + chunk * 2
            wall_ref[pl.ds(place, 8, stride=2 * PER), :] = jnp.where(used, vx * scale, 0.0)
            wall_ref[pl.ds(place + 1, 8, stride=2 * PER), :] = jnp.where(used, vz * scale, 0.0)

    for copy in copies:
        copy.wait()


VMEM = pl.BlockSpec(memory_space=pltpu.VMEM)
HBM = pl.BlockSpec(memory_space=pltpu.HBM)


def call(kernel, inputs, outputs, scratch=(), name=None, cost=1, specs=None, out_specs=None, limit=8, aliases={}):
    return pl.pallas_call(
        kernel,
        out_shape=[jax.ShapeDtypeStruct(shape, dtype) for shape, dtype in outputs],
        in_specs=specs or [VMEM] * len(inputs),
        out_specs=out_specs or [VMEM] * len(outputs),
        scratch_shapes=[s if not isinstance(s, tuple) else pltpu.VMEM(*s) for s in scratch],
        name=name,
        input_output_aliases=aliases,
        cost_estimate=pl.CostEstimate(flops=cost * 10**9, bytes_accessed=cost * 3 * 10**6, transcendentals=0),
        compiler_params=pltpu.CompilerParams(vmem_limit_bytes=int(limit * 1024 * 1024)),
    )(*inputs)


def exchange(axis, first, second, stage):
    count = lax.axis_size(axis)
    with jax.named_scope(stage + "_first"):
        one = lax.ppermute(first, axis, [(i, i + 1 - 2 * (i % 2)) for i in range(count)])
    with jax.named_scope(stage + "_second"):
        other = lax.ppermute(second, axis, [(i, (i - 1 + 2 * (i % 2)) % count) for i in range(count)])
    return one, other


def after(value, *others):
    return lax.optimization_barrier((value, *others))[0]


CUTS = (0, 8, 20, 32)
ENTROPY_LIMIT = 52


def local(flow_state, match_elem, match_coord, match_dest, roughness):
    faces = [((128, 128), F32), ((128, 128), F32), ((8, 128), F32), ((8, 128), F32)]
    nodal = ((256, 8, 128), F32)
    flow_rows = flow_state.transpose(1, 0, 2).reshape(5, 8, 8, 8, 128).transpose(0, 1, 3, 2, 4).reshape(5, 512, 128)
    dest = match_dest.reshape(64, 128)
    elem = match_elem.reshape(1, M_DEV)
    rough = roughness.reshape(N_WALL * PER, 128)
    v, table, x1, x2, z1, z2 = call(
        entropy_kernel,
        [flow_rows],
        [nodal, ((1536, 256), BF16)] + faces,
        [((5, 512, 128), F32), pltpu.SemaphoreType.DMA((4,))],
        name="entropy",
        specs=[HBM],
        limit=ENTROPY_LIMIT,
    )
    rank, hot = call(
        rank_kernel,
        [match_dest.reshape(1, M_DEV)],
        [((64, 128), jnp.int32), ((256, M_DEV), BF16)],
        [((2048, 128), BF16), ((2048, 256), F32)],
        name="rank",
    )
    probes = []
    for i, (first, last) in enumerate(zip(CUTS[:-1], CUTS[1:])):
        (probe,) = call(
            lambda *refs, first=first, last=last: probe_kernel(first, last, *refs),
            [after(table, probes[-1]) if probes else after(table, rank), elem, match_coord],
            [((4, (last - first) * PROBE_BLOCK // 128, 128), F32)],
            name=f"probe{i}",
            cost=5,
        )
        probes.append(probe)
    halos = [*exchange("slab", x1, after(x2, rank), "vx")]
    halos += exchange("wall", after(z1, probes[0]), after(z2, probes[1]), "vz")
    send, own = call(
        send_kernel,
        [*probes, after(rank, *halos), dest, hot, rough],
        [((N_WALL * CHUNK, 128), F32), ((3, 64, 128), F32)],
        [((576, M_DEV), BF16)],
        name="send",
        cost=3,
        limit=16,
    )
    got = lax.all_to_all(send.reshape(N_WALL, 1, CHUNK * 128), "wall", 0, 0, tiled=True)
    part, x1, x2, z1, z2 = call(
        flux_kernel,
        [after(v, send), *halos],
        [nodal] + faces,
        [((768, 8, 128), F32), ((576, 8, 128), F32)],
        name="flux",
        limit=12,
    )
    halos = [*exchange("slab", x1, x2, "fx"), *exchange("wall", z1, z2, "fz")]
    rate, bottom = call(
        assemble_kernel,
        [part, *halos],
        [((2048, 128), F32), ((64, 8, 128), F32)],
        [((2048, 128), F32), pltpu.SemaphoreType.DMA((4,))],
        name="assemble",
        out_specs=[HBM, VMEM],
    )
    rate, wall = call(
        final_kernel,
        [rate, bottom, got.reshape(N_WALL * CHUNK, 128), own, rank, dest, rough],
        [((2048, 128), F32), ((2 * N_WALL * PER, 128), F32)],
        [
            ((PER * N_WALL, 256), BF16),
            ((64, 128), F32),
            ((256, 128), F32),
            ((512, 128), F32),
            pltpu.SemaphoreType.DMA((4,)),
        ],
        name="final",
        specs=[HBM] + [VMEM] * 6,
        out_specs=[HBM, VMEM],
        aliases={0: 0},
    )
    rate = rate.reshape(64, 8, 4, 128).transpose(0, 2, 1, 3).reshape(64, 4, 1024)
    wall_shear = wall.reshape(N_WALL * PER, 2, 128).transpose(1, 0, 2).reshape(2, N_WALL * CAP)
    return (rate, wall_shear)


def solution(mesh):
    return jax.shard_map(
        local,
        mesh=mesh,
        in_specs=(
            P(None, None, ("slab", "wall")),
            P(("slab", "wall")),
            P(None, ("slab", "wall")),
            P(("slab", "wall"), None),
            P(("slab", "wall")),
        ),
        out_specs=(P(None, None, ("slab", "wall")), P(None, ("slab", "wall"))),
        check_vma=False,
    )
```

```python
import jax
import jax.numpy as jnp
import numpy as np
from jax import lax
from jax.experimental import pallas as pl
from jax.experimental.pallas import tpu as pltpu
from jax.sharding import PartitionSpec as P

EX = 4
EY = 2
EZ = 128
RES = 16
NEWTON = 8
CAP = 640
N_WALL = 32
M_DEV = 8192

VISCOSITY = 0.05
FOURIER_LAW_ON = 0.07 / 0.288
KARMAN = 0.41
RELAXATION = 0.35
F32 = jnp.float32
BF16 = jnp.bfloat16


def gauss_points():
    return np.array([-1.0, -1.0 / np.sqrt(5.0), 1.0 / np.sqrt(5.0), 1.0])


def derivative_matrix():
    points = gauss_points()
    bary = [
        1.0 / np.prod([points[i] - points[j] for j in range(4) if j != i]) for i in range(4)
    ]
    matrix = np.zeros((4, 4))
    for i in range(4):
        for j in range(4):
            if i != j:
                matrix[i, j] = bary[j] / bary[i] / (points[i] - points[j])
        matrix[i, i] = -np.sum(matrix[i])
    return matrix


D = derivative_matrix()
EVEN0 = float(0.5 * (D[0, 0] + D[0, 3]))
EVEN1 = float(0.5 * (D[1, 0] + D[1, 3]))
ODD00 = float(0.5 * (D[0, 0] - D[0, 3]))
ODD01 = float(0.5 * (D[0, 1] - D[0, 2]))
ODD10 = float(0.5 * (D[1, 0] - D[1, 3]))
ODD11 = float(0.5 * (D[1, 1] - D[1, 2]))


def line_derivative(u0, u1, u2, u3):
    even = (u0 + u3) - (u1 + u2)
    odd0 = u0 - u3
    odd1 = u1 - u2
    half0 = EVEN0 * even
    half1 = EVEN1 * even
    mean0 = ODD00 * odd0 + ODD01 * odd1
    mean1 = ODD10 * odd0 + ODD11 * odd1
    return mean0 + half0, mean1 + half1, mean1 - half1, mean0 - half0


def iota(shape, dim):
    return lax.broadcasted_iota(jnp.int32, shape, dim)


def entropy_of(rho, mx, my, mz, energy):
    inv_rho = 1.0 / rho
    speed_sq = mx * mx + my * my + mz * mz
    pressure = 0.4 * (energy - 0.5 * speed_sq * inv_rho)
    entropy_s = jnp.log(pressure) - 1.4 * jnp.log(rho)
    inv_p = 1.0 / pressure
    leading = (1.4 - entropy_s) / 0.4 - 0.5 * speed_sq * inv_rho * inv_p
    return leading, mx * inv_p, my * inv_p, mz * inv_p, -rho * inv_p


def line_nodes(direction, line):
    outer, inner = line // 4, line % 4
    if direction == 0:
        return [16 * a + 4 * outer + inner for a in range(4)]
    if direction == 1:
        return [16 * outer + 4 * b + inner for b in range(4)]
    return [16 * outer + 4 * inner + c for c in range(4)]


def is_even(axis):
    return lax.rem(lax.axis_index(axis), 2) == 0


def pick(condition, one, other):
    return lax.select(jnp.broadcast_to(condition, one.shape), one, other)


def pack_x(get_lower, get_upper, first_ref, second_ref):
    even = is_even("slab")
    pair = iota((8, 128), 0) // 2
    for block in range(16):
        upper = pltpu.roll(get_upper(4 * block), 2, 0)
        lower = get_lower(4 * block)
        for i in range(1, 4):
            upper = jnp.where(pair == i, pltpu.roll(get_upper(4 * block + i), (2 + 2 * i) % 8, 0), upper)
            lower = jnp.where(pair == i, pltpu.roll(get_lower(4 * block + i), 2 * i, 0), lower)
        first_ref[pl.ds(8 * block, 8), :] = pick(even, upper, lower)
        second_ref[pl.ds(8 * block, 8), :] = pick(even, lower, upper)


def pack_z(get_lower, get_upper):
    lane = iota((8, 128), 1)
    upper = jnp.zeros((8, 128), F32)
    lower = jnp.zeros((8, 128), F32)
    for k in range(64):
        upper = jnp.where(lane == k, pltpu.roll(get_upper(k), (k + 1) % 128, 1), upper)
        low = get_lower(k)
        lower = jnp.where(lane == k, low if k == 0 else pltpu.roll(low, k, 1), lower)
    return upper, lower


def x_halos(first_ref, second_ref, block):
    even = is_even("slab")
    first = first_ref[pl.ds(8 * block, 8), :]
    second = second_ref[pl.ds(8 * block, 8), :]
    return pick(even, second, first), pick(even, first, second)


def join_x(u, halos, i, row):
    prev_halo, next_halo = halos
    if i:
        prev_halo = pltpu.roll(prev_halo, 8 - 2 * i, 0)
    if i != 3:
        next_halo = pltpu.roll(next_halo, 6 - 2 * i, 0)
    prev = jnp.where(row < 2, prev_halo, pltpu.roll(u[3], 2, 0))
    following = jnp.where(row >= 6, next_halo, pltpu.roll(u[0], 6, 0))
    return prev, following


def entropy_kernel(flow_ref, v_ref, table_ref, x1_ref, x2_ref, z1_ref, z2_ref, rows_ref, sems):
    copies = [
        pltpu.make_async_copy(
            flow_ref.at[:, pl.ds(128 * part, 128), :], rows_ref.at[:, pl.ds(128 * part, 128), :], sems.at[part]
        )
        for part in range(4)
    ]
    for copy in copies:
        copy.start()
    for part in range(4):
        copies[part].wait()
        for n in range(16 * part, 16 * part + 16):
            start = n // 8 * 64 + n % 8
            values = entropy_of(*[rows_ref[c, pl.ds(start, 8, stride=8), :] for c in range(5)])
            for k in range(4):
                v_ref[k * 64 + n] = values[1 + k]
        for field, c in enumerate((0, 1, 3)):
            for j in range(8):
                value = jnp.concatenate(
                    [rows_ref[c, pl.ds(part * 128 + half * 64 + j * 8, 8), :] for half in range(2)], axis=0
                )
                high = value.astype(BF16)
                low = (value - high.astype(F32)).astype(BF16)
                base = j // 2 * 384 + field * 64 + part * 16
                lanes = pl.ds(j % 2 * 128, 128)
                table_ref[pl.ds(base, 16), lanes] = high
                table_ref[pl.ds(base + 192, 16), lanes] = low

    def face(direction, end):
        return lambda k: v_ref[(k // 16) * 64 + line_nodes(direction, k % 16)[end]]

    pack_x(face(0, 0), face(0, 3), x1_ref, x2_ref)
    upper, lower = pack_z(face(2, 0), face(2, 3))
    even = is_even("wall")
    z1_ref[...] = pick(even, upper, lower)
    z2_ref[...] = pick(even, lower, upper)


def jumps_y(lower, upper):
    odd = iota((8, 128), 0) % 2 == 1
    prev = jnp.where(odd, pltpu.roll(upper, 1, 0), lower)
    following = jnp.where(odd, upper, pltpu.roll(lower, 7, 0))
    return prev, following


FLUX = ((0, 1, 2, 6), (1, 3, 4, 7), (2, 4, 5, 8))


def flux_kernel(v_ref, x1_ref, x2_ref, z1_ref, z2_ref,
                rate_ref, fx1_ref, fx2_ref, fz1_ref, fz2_ref, g_ref, f_ref):
    row = iota((8, 128), 0)
    lane = iota((8, 128), 1)
    odd = row % 2 == 1
    even = is_even("wall")
    z_prev = pick(even, z2_ref[...], z1_ref[...])
    z_next = pick(even, z1_ref[...], z2_ref[...])

    for k in range(64):
        comp, line = k // 16, k % 16
        for direction in range(3):
            nodes = line_nodes(direction, line)
            u = [v_ref[comp * 64 + n] for n in nodes]
            d = list(line_derivative(*u))
            if direction == 0:
                prev, following = join_x(u, x_halos(x1_ref, x2_ref, k // 4), k % 4, row)
            elif direction == 1:
                prev, following = jumps_y(u[0], u[3])
            else:
                prev_halo = pltpu.roll(z_prev, 128 - k, 1) if k else z_prev
                next_halo = pltpu.roll(z_next, 127 - k, 1)
                prev = jnp.where(lane == 0, prev_halo, pltpu.roll(u[3], 1, 1))
                following = jnp.where(lane == 127, next_halo, pltpu.roll(u[0], 127, 1))
            d[0] = d[0] - 3.0 * (prev - u[0])
            d[3] = d[3] + 3.0 * (following - u[3])
            for end in range(4):
                g_ref[(direction * 4 + comp) * 64 + nodes[end]] = d[end]

    def pointwise(n, carry):
        v = [v_ref[c * 64 + n] for c in range(4)]
        g = [[g_ref[(d * 4 + c) * 64 + n] for c in range(4)] for d in range(3)]
        temperature = -1.0 / v[3]
        u = [v[i] * temperature for i in range(3)]
        scaled = VISCOSITY * temperature
        gu = [[scaled * (g[d][i] + u[i] * g[d][3]) for i in range(3)] for d in range(3)]
        third = (2.0 / 3.0) * (gu[0][0] + gu[1][1] + gu[2][2])
        conduct = FOURIER_LAW_ON * temperature * temperature
        tau = [[None] * 3 for _ in range(3)]
        for d in range(3):
            for i in range(d, 3):
                entry = gu[d][i] + gu[i][d]
                if i == d:
                    entry = entry - third
                tau[d][i] = entry
                tau[i][d] = entry
        for d in range(3):
            heat = u[0] * tau[d][0] + u[1] * tau[d][1] + u[2] * tau[d][2] + conduct * g[d][3]
            for c in range(d, 3):
                f_ref[FLUX[d][c] * 64 + n] = tau[d][c]
            f_ref[FLUX[d][3] * 64 + n] = heat
        return carry

    lax.fori_loop(0, 64, pointwise, 0, unroll=4)

    def face(direction, end):
        return lambda k: f_ref[FLUX[direction][k // 16] * 64 + line_nodes(direction, k % 16)[end]]

    pack_x(face(0, 0), face(0, 3), fx1_ref, fx2_ref)
    upper, lower = pack_z(face(2, 0), face(2, 3))
    fz1_ref[...] = pick(even, upper, lower)
    fz2_ref[...] = pick(even, lower, upper)

    for comp in range(4):
        for direction in range(3):
            for line in range(16):
                nodes = line_nodes(direction, line)
                u = [f_ref[FLUX[direction][comp] * 64 + n] for n in nodes]
                d = list(line_derivative(*u))
                if direction == 0:
                    prev = jnp.where(row < 2, 0.0, pltpu.roll(u[3], 2, 0))
                    following = jnp.where(row >= 6, 0.0, pltpu.roll(u[0], 6, 0))
                elif direction == 1:
                    prev, following = jumps_y(u[0], u[3])
                else:
                    prev = jnp.where(lane == 0, 0.0, pltpu.roll(u[3], 1, 1))
                    following = jnp.where(lane == 127, 0.0, pltpu.roll(u[0], 127, 1))
                d[0] = d[0] - 3.0 * (prev - u[0])
                d[3] = d[3] + 3.0 * (following - u[3])
                if direction == 1 and comp in (0, 2):
                    d[0] = d[0] + jnp.where(odd, 0.0, 6.0 * u[0])
                for end in range(4):
                    where = comp * 64 + nodes[end]
                    if direction == 0:
                        rate_ref[where] = d[end]
                    else:
                        rate_ref[where] = rate_ref[where] + d[end]


def assemble_kernel(part_ref, x1_ref, x2_ref, z1_ref, z2_ref, rate_ref, bottom_ref, out_ref, sems):
    row = iota((8, 128), 0)
    lane = iota((8, 128), 1)
    even = is_even("wall")
    z_prev = pick(even, z2_ref[...], z1_ref[...])
    z_next = pick(even, z1_ref[...], z2_ref[...])
    copies = []
    for n in range(64):
        a, b, c = n // 16, n // 4 % 4, n % 4
        for comp in range(4):
            total = part_ref[comp * 64 + n]
            if a in (0, 3):
                k = comp * 16 + 4 * b + c
                i = k % 4
                halo = x_halos(x1_ref, x2_ref, k // 4)[0 if a == 0 else 1]
                shift = (8 - 2 * i) % 8 if a == 0 else 6 - 2 * i
                if shift:
                    halo = pltpu.roll(halo, shift, 0)
                if a == 0:
                    total = total - jnp.where(row < 2, 3.0 * halo, 0.0)
                else:
                    total = total + jnp.where(row >= 6, 3.0 * halo, 0.0)
            if c in (0, 3):
                k = comp * 16 + 4 * a + b
                halo = z_prev if c == 0 else z_next
                shift = (128 - k) % 128 if c == 0 else 127 - k
                if shift:
                    halo = pltpu.roll(halo, shift, 1)
                if c == 0:
                    total = total - jnp.where(lane == 0, 3.0 * halo, 0.0)
                else:
                    total = total + jnp.where(lane == 127, 3.0 * halo, 0.0)
            if b == 0:
                bottom_ref[(4 * a + c) * 4 + comp] = total
            else:
                out_ref[pl.ds(n * 32 + comp, 8, stride=4), :] = total
        if n % 16 == 15:
            span = pl.ds(512 * a + 128, 384)
            copies.append(pltpu.make_async_copy(out_ref.at[span], rate_ref.at[span], sems.at[a]))
            copies[-1].start()
    for copy in copies:
        copy.wait()


def rank_kernel(dest_ref, rank_ref, hot_ref, named_ref, count_ref):
    before = (iota((128, 128), 0) < iota((128, 128), 1)).astype(F32).astype(BF16)
    counter = jnp.concatenate([before, jnp.ones((128, 128), BF16)], axis=1)
    wall_ids = iota((N_WALL, 128), 0)
    low_ids = iota((256, 128), 0).astype(jnp.int16)
    one, zero = jnp.ones((), BF16), jnp.zeros((), BF16)
    blocks = M_DEV // 128
    for block in range(blocks):
        named = (wall_ids == dest_ref[0:1, 128 * block : 128 * block + 128]).astype(F32).astype(BF16)
        named_ref[pl.ds(N_WALL * block, N_WALL), :] = named
    count_ref[...] = jnp.dot(named_ref[...], counter, preferred_element_type=F32)
    total = jnp.zeros((N_WALL, 128), F32)
    for block in range(blocks):
        rows = pl.ds(N_WALL * block, N_WALL)
        lanes = pl.ds(128 * block, 128)
        own = wall_ids == dest_ref[0:1, 128 * block : 128 * block + 128]
        rank = jnp.sum(jnp.where(own, count_ref[rows, :128] + total, 0.0), axis=0, keepdims=True).astype(jnp.int32)
        rank_ref[pl.ds(block, 1), :] = rank
        low = jnp.broadcast_to(rank & 255, (256, 128)).astype(jnp.int16)
        hot_ref[:, lanes] = jnp.where(low_ids == low, one, zero)
        total = total + count_ref[rows, 128:]


PROBE_BLOCK = 256


def probe_kernel(first, last, table_ref, elem_ref, coord_ref, probe_ref):
    points = gauss_points()
    width = PROBE_BLOCK
    scales = [float(1.0 / np.prod([points[i] - points[j] for j in range(4) if j != i])) for i in range(4)]

    def basis_rows(coordinate, index):
        if isinstance(index, int):
            product = scales[index]
            for other in range(4):
                if other != index:
                    product = product * (coordinate - float(points[other]))
            return product
        product = jnp.where(
            index == 0, scales[0], jnp.where(index == 1, scales[1], jnp.where(index == 2, scales[2], scales[3]))
        )
        for other in range(4):
            product = product * jnp.where(index == other, 1.0, coordinate - float(points[other]))
        return product

    low_ids = iota((256, width), 0)
    row16 = iota((16, width), 0)

    def probe_block(block, carry):
        here = pl.ds(pl.multiple_of(block * width, width), width)
        elem = elem_ref[0:1, here]
        hot = (low_ids == elem & 255).astype(F32).astype(BF16)
        picked = jnp.dot(table_ref[...], hot, preferred_element_type=F32).reshape(4, 2, 24, 8, width)
        group = jnp.broadcast_to(elem >> 8, (8, width))
        both = picked[:, 0] + picked[:, 1]
        values = both[0]
        for g in range(1, 4):
            values = jnp.where((group == g)[None], both[g], values)
        values = values.reshape(192, width)
        coords = [(2.0 * coord_ref[d : d + 1, here].astype(F32) + 1.0) / RES - 1.0 for d in range(3)]
        wide = [jnp.broadcast_to(coords[d], (16, width)) for d in range(3)]
        along_yz = basis_rows(wide[1], row16 // 4) * basis_rows(wide[2], row16 % 4)
        along_x = [basis_rows(wide[0], a) for a in range(4)]
        results = []
        for field in range(3):
            total = None
            for a in range(4):
                term = along_x[a] * values[64 * field + 16 * a : 64 * field + 16 * a + 16]
                total = term if total is None else total + term
            results.append(jnp.sum(total * along_yz, axis=0, keepdims=True))
        layer = (elem // EZ % EY).astype(F32)
        results.append(2.0 * layer + 1.0 + coords[1])
        for field in range(4):
            for i in range(width // 128):
                probe_ref[field, pl.ds((block - first) * (width // 128) + i, 1), :] = results[field][
                    :, 128 * i : 128 * (i + 1)
                ]
        return carry

    lax.fori_loop(first, last, probe_block, 0, unroll=4)


SEND_BLOCK = 1024
PER = CAP // 128
CHUNK = 4 * PER


def send_kernel(*refs):
    n_probe = len(refs) - 7
    probe_refs = refs[:n_probe]
    rank_ref, dest_ref, hot_ref, rough_ref, send_ref, own_ref, lhs_ref = refs[n_probe:]
    rows = M_DEV // 128
    rho, mx, mz, height = [jnp.concatenate([ref[f] for ref in probe_refs], axis=0) for f in range(4)]
    inv_rho = 1.0 / rho
    vel_x = mx * inv_rho
    vel_z = mz * inv_rho
    slip = jnp.maximum(jnp.sqrt(vel_x * vel_x + vel_z * vel_z), 0.5)
    values = [slip * mx, slip * mz, height * slip * rho * (1.0 / VISCOSITY)]
    parts = []
    for f in range(3):
        own_ref[f] = values[f]
        high = values[f].astype(BF16).astype(F32)
        parts += [high, values[f] - high]

    code = (rank_ref[...] // 256) * N_WALL + dest_ref[...]
    code_ids = iota((96, 128), 0).astype(jnp.int16)
    zero = jnp.zeros((), BF16)
    total = jnp.zeros((576, 256), F32)
    per = SEND_BLOCK // 128
    for block in range(M_DEV // SEND_BLOCK):
        for i in range(per):
            r = block * per + i
            match = code_ids == jnp.broadcast_to(code[r : r + 1], (96, 128)).astype(jnp.int16)
            for part in range(6):
                value = jnp.broadcast_to(parts[part][r : r + 1], (96, 128)).astype(BF16)
                lhs_ref[pl.ds(96 * part, 96), pl.ds(128 * r, 128)] = jnp.where(match, value, zero)
        span = pl.ds(block * SEND_BLOCK, SEND_BLOCK)
        total = total + lax.dot_general(
            lhs_ref[:, span], hot_ref[:, span], (((1,), (1,)), ((), ())), preferred_element_type=F32
        )
    for chunk in range(PER):
        q, half = chunk // 2, chunk % 2
        lanes = slice(128 * half, 128 * half + 128)
        for w in range(0, N_WALL, 8):
            for f in range(3):
                base = 192 * f + q * N_WALL + w
                send_ref[pl.ds(w * CHUNK + f * PER + chunk, 8, stride=CHUNK), :] = (
                    total[base : base + 8, lanes] + total[base + 96 : base + 104, lanes]
                )
            send_ref[pl.ds(w * CHUNK + 3 * PER + chunk, 8, stride=CHUNK), :] = rough_ref[
                pl.ds(w * PER + chunk, 8, stride=PER), :
            ]


def shear_scale(log_term):
    ratio = jnp.ones_like(log_term)
    for sweep in range(NEWTON):
        numerator = KARMAN * ratio - log_term + jnp.log(ratio)
        ratio = ratio - RELAXATION * ratio * numerator / (KARMAN * ratio + 1.0)
    return 1.0 / (ratio * ratio)


def final_kernel(kept_ref, bottom_ref, got_ref, own_ref, rank_ref, dest_ref, rough_ref,
                 rate_ref, wall_ref, table_ref, factor_ref, shear_ref, out_ref, sems):
    for chunk in range(PER):
        for w in range(0, N_WALL, 16):
            value = jnp.concatenate(
                [got_ref[pl.ds((w + 8 * i) * CHUNK + 3 * PER + chunk, 8, stride=CHUNK), :] for i in range(2)], axis=0
            )
            high = value.astype(BF16)
            table_ref[pl.ds(chunk * N_WALL + w, 16), :128] = high
            table_ref[pl.ds(chunk * N_WALL + w, 16), 128:] = (value - high.astype(F32)).astype(BF16)
    code = (rank_ref[...] >> 7) * N_WALL + dest_ref[...]
    code_ids = iota((PER * N_WALL, 128), 0)
    ids = iota((128, 512), 0).astype(jnp.int16)
    one, zero = jnp.ones((), BF16), jnp.zeros((), BF16)
    for block in range(M_DEV // 512):
        place = jnp.concatenate([rank_ref[r : r + 1, :] & 127 for r in range(4 * block, 4 * block + 4)], axis=1)
        hot = jnp.where(ids == jnp.broadcast_to(place, (128, 512)).astype(jnp.int16), one, zero)
        found = jnp.dot(table_ref[...], jnp.concatenate([hot, hot], axis=0), preferred_element_type=F32)
        for i in range(4):
            r = 4 * block + i
            picked = jnp.where(code_ids == code[r : r + 1], found[:, 128 * i : 128 * i + 128], 0.0)
            factor_ref[pl.ds(r, 1), :] = jnp.sum(picked, axis=0, keepdims=True)
    scale = shear_scale(jnp.log(factor_ref[...] * own_ref[2]))
    shear_ref[...] = jnp.zeros_like(shear_ref)
    for comp in range(2):
        shear = own_ref[comp] * scale
        for pair in range(16):
            shear_ref[pl.ds(128 * comp + 8 * pair, 4, stride=2), :] = shear[4 * pair : 4 * pair + 4]
    copies = []
    for a in range(4):
        for c in range(4):
            for comp in range(4):
                total = bottom_ref[(4 * a + c) * 4 + comp]
                if comp in (0, 2):
                    total = total - 6.0 * shear_ref[pl.ds((comp // 2) * 128 + (4 * a + c) * 8, 8), :]
                out_ref[pl.ds(128 * a + 32 * c + comp, 8, stride=4), :] = total
        copies.append(
            pltpu.make_async_copy(out_ref.at[pl.ds(128 * a, 128)], rate_ref.at[pl.ds(512 * a, 128)], sems.at[a])
        )
        copies[-1].start()

    for chunk in range(PER):
        for w in range(0, N_WALL, 8):
            vx, vz, reynolds = [
                got_ref[pl.ds(w * CHUNK + f * PER + chunk, 8, stride=CHUNK), :] for f in range(3)
            ]
            used = reynolds > 0.0
            factor = rough_ref[pl.ds(w * PER + chunk, 8, stride=PER), :]
            scale = shear_scale(jnp.log(factor * jnp.where(used, reynolds, 1.0)))
            place = w * PER * 2 + chunk * 2
            wall_ref[pl.ds(place, 8, stride=2 * PER), :] = jnp.where(used, vx * scale, 0.0)
            wall_ref[pl.ds(place + 1, 8, stride=2 * PER), :] = jnp.where(used, vz * scale, 0.0)

    for copy in copies:
        copy.wait()


VMEM = pl.BlockSpec(memory_space=pltpu.VMEM)
HBM = pl.BlockSpec(memory_space=pltpu.HBM)


def call(kernel, inputs, outputs, scratch=(), name=None, cost=1, specs=None, out_specs=None, limit=8, aliases={}):
    return pl.pallas_call(
        kernel,
        out_shape=[jax.ShapeDtypeStruct(shape, dtype) for shape, dtype in outputs],
        in_specs=specs or [VMEM] * len(inputs),
        out_specs=out_specs or [VMEM] * len(outputs),
        scratch_shapes=[s if not isinstance(s, tuple) else pltpu.VMEM(*s) for s in scratch],
        name=name,
        input_output_aliases=aliases,
        cost_estimate=pl.CostEstimate(flops=cost * 10**9, bytes_accessed=cost * 3 * 10**6, transcendentals=0),
        compiler_params=pltpu.CompilerParams(vmem_limit_bytes=int(limit * 1024 * 1024)),
    )(*inputs)


def exchange(axis, first, second, stage):
    count = lax.axis_size(axis)
    with jax.named_scope(stage + "_first"):
        one = lax.ppermute(first, axis, [(i, i + 1 - 2 * (i % 2)) for i in range(count)])
    with jax.named_scope(stage + "_second"):
        other = lax.ppermute(second, axis, [(i, (i - 1 + 2 * (i % 2)) % count) for i in range(count)])
    return one, other


def after(value, *others):
    return lax.optimization_barrier((value, *others))[0]


CUTS = (0, 8, 20, 32)
ENTROPY_LIMIT = 52


def local(flow_state, match_elem, match_coord, match_dest, roughness):
    faces = [((128, 128), F32), ((128, 128), F32), ((8, 128), F32), ((8, 128), F32)]
    nodal = ((256, 8, 128), F32)
    flow_rows = flow_state.transpose(1, 0, 2).reshape(5, 8, 8, 8, 128).transpose(0, 1, 3, 2, 4).reshape(5, 512, 128)
    dest = match_dest.reshape(64, 128)
    elem = match_elem.reshape(1, M_DEV)
    rough = roughness.reshape(N_WALL * PER, 128)
    v, table, x1, x2, z1, z2 = call(
        entropy_kernel,
        [flow_rows],
        [nodal, ((1536, 256), BF16)] + faces,
        [((5, 512, 128), F32), pltpu.SemaphoreType.DMA((4,))],
        name="entropy",
        specs=[HBM],
        limit=ENTROPY_LIMIT,
    )
    rank, hot = call(
        rank_kernel,
        [match_dest.reshape(1, M_DEV)],
        [((64, 128), jnp.int32), ((256, M_DEV), BF16)],
        [((2048, 128), BF16), ((2048, 256), F32)],
        name="rank",
    )
    probes = []
    for i, (first, last) in enumerate(zip(CUTS[:-1], CUTS[1:])):
        (probe,) = call(
            lambda *refs, first=first, last=last: probe_kernel(first, last, *refs),
            [after(table, probes[-1]) if probes else after(table, rank), elem, match_coord],
            [((4, (last - first) * PROBE_BLOCK // 128, 128), F32)],
            name=f"probe{i}",
            cost=5,
        )
        probes.append(probe)
    halos = [*exchange("slab", x1, after(x2, rank), "vx")]
    halos += exchange("wall", after(z1, probes[0]), after(z2, probes[1]), "vz")
    send, own = call(
        send_kernel,
        [*probes, after(rank, *halos), dest, hot, rough],
        [((N_WALL * CHUNK, 128), F32), ((3, 64, 128), F32)],
        [((576, M_DEV), BF16)],
        name="send",
        cost=3,
        limit=16,
    )
    got = lax.all_to_all(send.reshape(N_WALL, 1, CHUNK * 128), "wall", 0, 0, tiled=True)
    part, x1, x2, z1, z2 = call(
        flux_kernel,
        [after(v, send), *halos],
        [nodal] + faces,
        [((768, 8, 128), F32), ((576, 8, 128), F32)],
        name="flux",
        limit=12,
    )
    halos = [*exchange("slab", x1, x2, "fx"), *exchange("wall", z1, z2, "fz")]
    rate, bottom = call(
        assemble_kernel,
        [part, *halos],
        [((2048, 128), F32), ((64, 8, 128), F32)],
        [((2048, 128), F32), pltpu.SemaphoreType.DMA((4,))],
        name="assemble",
        out_specs=[HBM, VMEM],
    )
    rate, wall = call(
        final_kernel,
        [rate, bottom, got.reshape(N_WALL * CHUNK, 128), own, rank, dest, rough],
        [((2048, 128), F32), ((2 * N_WALL * PER, 128), F32)],
        [
            ((PER * N_WALL, 256), BF16),
            ((64, 128), F32),
            ((256, 128), F32),
            ((512, 128), F32),
            pltpu.SemaphoreType.DMA((4,)),
        ],
        name="final",
        specs=[HBM] + [VMEM] * 6,
        out_specs=[HBM, VMEM],
        aliases={0: 0},
    )
    rate = rate.reshape(64, 8, 4, 128).transpose(0, 2, 1, 3).reshape(64, 4, 1024)
    wall_shear = wall.reshape(N_WALL * PER, 2, 128).transpose(1, 0, 2).reshape(2, N_WALL * CAP)
    return (rate, wall_shear)


def solution(mesh):
    return jax.shard_map(
        local,
        mesh=mesh,
        in_specs=(
            P(None, None, ("slab", "wall")),
            P(("slab", "wall")),
            P(None, ("slab", "wall")),
            P(("slab", "wall"), None),
            P(("slab", "wall")),
        ),
        out_specs=(P(None, None, ("slab", "wall")), P(None, ("slab", "wall"))),
        check_vma=False,
    )
```
